128 devices in a mesh: group: 16 (over y, x), expert: 8 (over z, core).
Axes of the slice: x: 4, y: 4, z: 4, core: 2. Of those that a mesh axis runs over, the one named last changes fastest.
Arguments:
- tokens_in: bfloat16 [16384, 2048], P(('group', 'expert')), may hold values from -6 to 6
- out_grad: bfloat16 [16384, 2048], P(('group', 'expert')), may hold values from -3 to 3
- expert_ids: int32 [16384, 8], P(('group', 'expert')), may hold values from 0 to 127, as said below
- gate_weights: float32 [16384, 8], P(('group', 'expert')), may hold values from 0.05 to 1
- w_gate: bfloat16 [128, 2048, 768], P(('group', 'expert')), may hold values from -0.125 to 0.125
- w_up: bfloat16 [128, 2048, 768], P(('group', 'expert')), may hold values from -0.125 to 0.125
- w_down: bfloat16 [128, 768, 2048], P(('group', 'expert')), may hold values from -0.21875 to 0.21875
Outputs:
- grad_in: bfloat16 [16384, 2048], P(('group', 'expert'))
- grad_gate: bfloat16 [128, 2048, 768], P(('group', 'expert'))
- grad_up: bfloat16 [128, 2048, 768], P(('group', 'expert'))
- grad_down: bfloat16 [128, 768, 2048], P(('group', 'expert'))
The draws below stay inside these ranges and needn't reach their ends.
Inputs may be any that keep to these rules, and one draw needn't show every extreme that they name: `expert_ids`: each row names 8 different experts. Among the 128 tokens of one device no expert is named more than 16 times, and some expert is named exactly 16 times by the tokens of some device. The tokens of one device name the experts of each group (experts g * 8 to g * 8 + 7) exactly 64 times. Over all 16384 tokens every expert is named exactly 128 * 8 times.
All inputs are finite; a program needn't handle non-finite values.
Results may differ from the reference program's by a relative error of at most 0.0065.
Values may be sent and summed in bfloat16 or wider, within the bound.
A program may use at most 128 MiB of HBM per device.

```python
import math
import jax
import jax.numpy as jnp
from jax import lax

D = 2048
FF = 768
TOP = 8
TOK_DEV = 128
EXPERTS = 128
TOKENS = 16384
CAP = 16
N_GROUP = 16
N_EXPERT = 8


def base_counts(key, half):
    rough = jax.random.randint(key, (N_GROUP, N_EXPERT // 2), 0, half + 1).at[0, 0].set(half)
    return jnp.concatenate([rough, half - rough], axis=1).astype(jnp.int32)


def spread_counts(base, order):
    group_shift = order // N_EXPERT
    owner_shift = order % N_EXPERT
    group_cols = jnp.arange(N_GROUP, dtype=jnp.int32)
    owner_cols = jnp.arange(N_EXPERT, dtype=jnp.int32)
    group_pick = (group_cols[None, :] + group_shift[:, None]) % N_GROUP
    owner_pick = (owner_cols[None, :] + owner_shift[:, None]) % N_EXPERT
    return base[group_pick[:, :, None], owner_pick[:, None, :]].reshape(EXPERTS, EXPERTS)


def draw_expert_ids(key, part):
    half = CAP // 2
    keys = jax.random.split(jax.random.fold_in(key, 7), 5)
    first_base = base_counts(keys[0], half)
    second_base = base_counts(keys[1], half)
    order_one = jax.random.permutation(keys[2], EXPERTS).astype(jnp.int32)
    mapping = jnp.concatenate([jnp.zeros((1,), jnp.int32), 1 + jax.random.permutation(keys[3], EXPERTS - 1).astype(jnp.int32)])
    order_two = order_one[mapping]
    block_counts = spread_counts(first_base, order_one) + spread_counts(second_base, order_two)
    block_ends = jnp.cumsum(block_counts, axis=1)
    occurrence = jnp.arange(TOK_DEV * TOP, dtype=jnp.int32)
    expert_of = jax.vmap(lambda ends_row: jnp.searchsorted(ends_row, occurrence, side='right'))(block_ends).astype(jnp.int32)
    table = jnp.transpose(expert_of.reshape(EXPERTS, TOP, TOK_DEV), (0, 2, 1))
    shuffles = jax.vmap(lambda sub_key: jax.random.permutation(sub_key, TOK_DEV))(jax.random.split(keys[4], EXPERTS)).astype(jnp.int32)
    table = jnp.take_along_axis(table, shuffles[:, :, None], axis=1)
    return table.reshape(TOKENS, TOP).astype(jnp.int32)


def shard_levels(stream_key, extent, cuts, smallest, largest):
    loudness = 1.0
    for position, shards_of in cuts:
        draws = jax.random.uniform(jax.random.fold_in(jax.random.fold_in(stream_key, 6), position), (shards_of,), jnp.float32, smallest / len(cuts), largest / len(cuts))
        loudness = loudness * jnp.repeat(jnp.exp(draws), extent[position] // shards_of).reshape((-1,) + (1,) * (len(extent) - 1 - position))
    return loudness


def centred(key, extent, spread, bound, pieces=(), kind=jnp.bfloat16):
    drawn = spread * jax.random.normal(key, extent, jnp.float32)
    if pieces:
        drawn = drawn * shard_levels(key, extent, pieces, -0.22, 0.18)
    return jnp.clip(drawn, -bound, bound).astype(kind)


def setup_inputs(seed: int = 0) -> dict:
    key_of = jax.random.split(jax.random.key(seed), 8)
    tokens_in = centred(key_of[0], (TOKENS, D), 1.0, 6.0, ((0, 128),))
    out_grad = centred(key_of[1], (TOKENS, D), 0.5, 3.0, ((0, 128),))
    expert_ids = draw_expert_ids(jax.random.fold_in(key_of[7], 71), 0)
    gate_weights = jnp.clip(jnp.exp(math.log(1.0) - 2.9957323 * jax.random.uniform(key_of[3], (TOKENS, TOP), jnp.float32) ** shard_levels(key_of[3], (TOKENS, TOP), ((0, 128),), -0.2, 0.2)), 0.05, 1.0)
    w_gate = centred(key_of[4], (EXPERTS, D, FF), D ** -0.5, 0.125, ((0, 128),))
    w_up = centred(key_of[5], (EXPERTS, D, FF), D ** -0.5, 0.125, ((0, 128),))
    w_down = centred(key_of[6], (EXPERTS, FF, D), FF ** -0.5, 0.21875, ((0, 128),))
    return {"tokens_in": tokens_in, "out_grad": out_grad, "expert_ids": expert_ids, "gate_weights": gate_weights, "w_gate": w_gate, "w_up": w_up, "w_down": w_down}


def contract_rows(first_op, second_op):
    return lax.dot_general(first_op, second_op, (((0,), (0,)), ((), ())), preferred_element_type=jnp.float32)


def contract_cols(first_op, second_op):
    return lax.dot_general(first_op, second_op, (((1,), (1,)), ((), ())), preferred_element_type=jnp.float32)


def expert_backward(inputs, grad_rows, gate_mat, up_mat, down_mat):
    gate_pre = jnp.dot(inputs, gate_mat, preferred_element_type=jnp.float32)
    up_pre = jnp.dot(inputs, up_mat, preferred_element_type=jnp.float32)
    sigma_gate = jax.nn.sigmoid(gate_pre)
    activated = gate_pre * sigma_gate
    hidden = (activated * up_pre).astype(jnp.bfloat16)
    hidden_grad = contract_cols(grad_rows, down_mat)
    down_grad = contract_rows(hidden, grad_rows).astype(jnp.bfloat16)
    gate_grad_rows = (hidden_grad * up_pre * sigma_gate * (1.0 + gate_pre * (1.0 - sigma_gate))).astype(jnp.bfloat16)
    up_grad_rows = (hidden_grad * activated).astype(jnp.bfloat16)
    input_rows = (contract_cols(gate_grad_rows, gate_mat) + contract_cols(up_grad_rows, up_mat)).astype(jnp.bfloat16)
    gate_weight_grad = contract_rows(inputs, gate_grad_rows).astype(jnp.bfloat16)
    up_weight_grad = contract_rows(inputs, up_grad_rows).astype(jnp.bfloat16)
    return gate_weight_grad, up_weight_grad, down_grad, input_rows


def reference(tokens_in, out_grad, expert_ids, gate_weights, w_gate, w_up, w_down):
    flat_ids = expert_ids.reshape(-1).astype(jnp.int32)
    sorted_rows = jnp.argsort(flat_ids, stable=True).astype(jnp.int32).reshape(EXPERTS, TOK_DEV * TOP)
    gate_flat = gate_weights.reshape(-1)

    def per_expert(summed, packed):
        pair_rows, gate_mat, up_mat, down_mat = packed
        token_rows = (pair_rows // TOP).astype(jnp.int32)
        inputs = tokens_in[token_rows]
        grad_rows = (gate_flat[pair_rows][:, None] * out_grad[token_rows].astype(jnp.float32)).astype(jnp.bfloat16)
        gate_g, up_g, down_g, input_rows = expert_backward(inputs, grad_rows, gate_mat, up_mat, down_mat)
        summed = summed.at[token_rows].add(input_rows.astype(jnp.float32))
        return summed, (gate_g, up_g, down_g)

    start_sum = jnp.zeros((TOKENS, D), jnp.float32)
    summed, grads = lax.scan(per_expert, start_sum, (sorted_rows, w_gate, w_up, w_down))
    return summed.astype(jnp.bfloat16), grads[0], grads[1], grads[2]
```

```python
import jax
import jax.numpy as jnp
from jax import lax
from jax.experimental import pallas as pl
from jax.experimental.pallas import tpu as pltpu
from jax.sharding import PartitionSpec as P

NG, NJ = 16, 8
T, D, FF = 128, 2048, 768
CAP = 16
PG = 64
E = NG * NJ
ROWS = NG * NJ * CAP
BF, F32, I32 = jnp.bfloat16, jnp.float32, jnp.int32
MESH = pl.DeviceIdType.MESH
VMEM_LIMIT = 67043328


def dot(a, b, ca=1, cb=0):
    return lax.dot_general(a, b, (((ca,), (cb,)), ((), ())), preferred_element_type=F32)


def shift_of(d):
    if isinstance(d, int):
        return d % 4, (d // 4 + d % 4) % 4
    dy = lax.rem(d, 4)
    return dy, lax.rem(lax.div(d, 4) + dy, 4)


def group_to(grp, d):
    dy, dx = shift_of(d)
    return lax.rem(lax.div(grp, 4) + dy, 4) * 4 + lax.rem(lax.rem(grp, 4) + dx, 4)


def group_from(grp, d):
    dy, dx = shift_of(d)
    return lax.rem(lax.div(grp, 4) - dy + 4, 4) * 4 + lax.rem(lax.rem(grp, 4) - dx + 4, 4)


def enter(grp, own):
    barrier = pltpu.get_barrier_semaphore()
    for d in range(1, NG):
        pl.semaphore_signal(barrier, inc=1, device_id=(group_to(grp, d), own), device_id_type=MESH)
    for k in range(1, NJ):
        pl.semaphore_signal(
            barrier, inc=1, device_id=(grp, lax.rem(own + k, NJ)), device_id_type=MESH
        )
    return barrier


def send(src, dst, ssem, rsem, device):
    pltpu.make_async_remote_copy(
        src_ref=src, dst_ref=dst, send_sem=ssem, recv_sem=rsem,
        device_id=device, device_id_type=MESH,
    ).start()


def landed(ref, sem):
    pltpu.make_async_copy(ref, ref, sem).wait()


def iota(shape, dim):
    return lax.broadcasted_iota(I32, shape, dim)


def dispatch_kernel(
    ids_ref, gw_ref, x_hbm, g_ref, wg_hbm, wu_hbm, wd_hbm,
    xr, gr, hid_o, gg_o, ug_o, c_o, pos_o,
    ax, pbuf, s1, r1, s2, stx, stg, wg, wu, wd, ost,
    rank_s, rank_r, pos_s, pos_r, post, wt,
    axs, axr, ms, mr, ps, pr, q1s, q1r, q2s, q2r, p2s, p2r, wsem, xsem, gsem, osem,
):
    grp, own = lax.axis_index("group"), lax.axis_index("expert")
    partner = own + 1 - 2 * lax.rem(own, 2)
    barrier = enter(grp, own)
    loads = [
        pltpu.make_async_copy(wg_hbm, wg, wsem.at[0]),
        pltpu.make_async_copy(wu_hbm, wu, wsem.at[1]),
        pltpu.make_async_copy(wd_hbm, wd, wsem.at[2]),
    ]
    pltpu.make_async_copy(x_hbm, ax.at[own], axr.at[own]).start()

    row, lane = iota((E, T), 0), iota((E, T), 1)
    before = jnp.where(row < lane, 1.0, 0.0).astype(BF)
    named = jnp.zeros((E, T), F32)
    weight = jnp.zeros((E, T), F32)
    named_p = jnp.zeros((E, T), F32)
    row_p = lax.rem(row, NG) * NJ + lax.div(row, NG)
    for k in range(8):
        idk = ids_ref[k : k + 1, :]
        gwk = gw_ref[k : k + 1, :]
        named = jnp.where(row == idk, 1.0, named)
        weight = jnp.where(row == idk, gwk, weight)
        named_p = jnp.where(row_p == idk, 1.0, named_p)
    rank = dot(named.astype(BF), before)
    rank_p = dot(named_p.astype(BF), before)
    counts = dot(named.astype(BF), jnp.ones((T, T), BF))
    ahead = jnp.where(
        (lax.div(row, NJ) == lax.div(lane, NJ)) & (lane < row), 1.0, 0.0
    ).astype(BF)
    starts = dot(ahead, counts.astype(BF))
    post[...] = jnp.where(named > 0.5, starts + rank, -1.0).astype(I32)
    wt[...] = weight
    rank_s[...] = jnp.where(named_p > 0.5, rank_p, -1.0).astype(I32).reshape(NJ, NG, T)
    mine = lax.rem(row, NJ) == lax.div(lane, CAP)
    pick = jnp.where(lax.div(iota((NG, E), 1), NJ) == iota((NG, E), 0), 1.0, 0.0).astype(BF)
    start_row = dot(pick, jnp.where(mine, starts, 0.0).astype(BF))
    count_row = dot(pick, jnp.where(mine, counts, 0.0).astype(BF))
    slot = lax.rem(iota((NG, E), 1), CAP).astype(F32)
    pos = jnp.where(slot < count_row, start_row + slot, -1.0).astype(I32)
    for a in range(NG):
        pos_s[a] = jnp.broadcast_to(pos[a : a + 1, :], (8, 128))
    rank_r[own] = rank_s[own]
    pos_r[grp] = pos_s[grp]

    pl.semaphore_wait(barrier, NG + NJ - 2)

    for k in range(1, NJ):
        to = lax.rem(own + k, NJ)
        send(rank_s.at[to], rank_r.at[own], ms.at[k], mr.at[own], (grp, to))
    for i in range(1, 4):
        to = lax.rem(own + 2 * i, NJ)
        send(x_hbm, ax.at[own], axs.at[i], axr.at[own], (grp, to))
    send(x_hbm, ax.at[own], axs.at[0], axr.at[own], (grp, partner))

    spot = iota((PG, T), 0)
    for b in range(4):
        picks, scales = [], []
        for q in range(4):
            a = group_to(grp, 4 * b + q)
            at = pl.ds(pl.multiple_of(a * NJ, NJ), NJ)
            prow, wrow = post[at, :], wt[at, :]
            hot = jnp.zeros((PG, T), F32)
            wsel = jnp.zeros((PG, T), F32)
            for e in range(NJ):
                hit = spot == prow[e : e + 1, :]
                hot = jnp.where(hit, 1.0, hot)
                wsel = jnp.where(hit, wrow[e : e + 1, :], wsel)
            c_o[pl.ds(pl.multiple_of(a * PG, PG), PG), :] = hot.astype(BF)
            picks.append(hot.astype(BF))
            scales.append(jnp.sum(wsel, axis=1, keepdims=True))
        hots = jnp.concatenate(picks, axis=0)
        scale = jnp.concatenate(scales, axis=0)
        for c in range(0, D, 512):
            part = (scale * dot(hots, g_ref[:, c : c + 512])).astype(BF)
            for q in range(4):
                s1[group_to(grp, 4 * b + q), :, c : c + 512] = part[q * PG : (q + 1) * PG, :]
        for q in range(4):
            d = 4 * b + q
            if d == 0:
                continue
            a = group_to(grp, d)
            send(pos_s.at[a], pos_r.at[grp], ps.at[d], pr.at[grp], (a, own))
            send(s1.at[a], r1.at[grp], q1s.at[d], q1r.at[grp], (a, own))
    for w in loads:
        w.start()

    def spread(a, rows_ref):
        hot = jnp.where(spot == pos_r[a, 0:1, :], 1.0, 0.0).astype(BF)
        for c in range(0, D, 512):
            s2[a, :, c : c + 512] = dot(hot, rows_ref[a, :, c : c + 512], 0, 0).astype(BF)
        for k in range(1, NJ):
            to = lax.rem(own + k, NJ)
            at = pl.ds(pl.multiple_of(to * CAP, CAP), CAP)
            send(s2.at[a, at], gr.at[a, own], q2s.at[a], q2r.at[a], (grp, to))
        at = pl.ds(pl.multiple_of(own * CAP, CAP), CAP)
        pltpu.make_async_copy(s2.at[a, at], gr.at[a, own], q2r.at[a]).start()

    spread(grp, s1)

    for i in range(1, 4):
        slot_i = lax.rem(own - 2 * i + NJ, NJ)
        landed(ax.at[slot_i], axr.at[slot_i])
        send(ax.at[slot_i], ax.at[slot_i], axs.at[3 + i], axr.at[slot_i], (grp, partner))
    for i in range(4):
        slot_i = lax.rem(partner + 2 * i, NJ)
        landed(ax.at[slot_i], axr.at[slot_i])
    landed(ax.at[own], axr.at[own])
    for k in range(1, NJ):
        frm = lax.rem(own + k, NJ)
        landed(rank_r.at[frm], mr.at[frm])

    cap_row = iota((CAP, T), 0)

    @pl.loop(0, NJ)
    def _(j):
        hots = jnp.concatenate(
            [
                jnp.where(cap_row == rank_r[j, a : a + 1, :], 1.0, 0.0).astype(BF)
                for a in range(NG)
            ],
            axis=0,
        )
        for c in range(0, D, 512):
            part = dot(hots, ax[j, :, c : c + 512]).astype(BF)
            pbuf[:, j, :, c : c + 512] = part.reshape(NG, CAP, 512)

    for d in range(1, NG):
        a = group_to(grp, d)
        send(pbuf.at[a], xr.at[grp], p2s.at[d], p2r.at[grp], (a, own))
    pltpu.make_async_copy(pbuf.at[grp], xr.at[grp], p2r.at[grp]).start()

    @pl.loop(1, NG)
    def _(d):
        a = group_from(grp, d)
        landed(pos_r.at[a], pr.at[a])
        landed(r1.at[a], q1r.at[a])
        spread(a, r1)

    for w in loads:
        w.wait()

    def fetch(i, s):
        for h in range(2):
            a = group_from(grp, 2 * i + h)
            landed(xr.at[a], p2r.at[a])
            landed(gr.at[a], q2r.at[a])
            pltpu.make_async_copy(xr.at[a], stx.at[s, pl.ds(h * NJ, NJ)], xsem.at[s]).start()
            pltpu.make_async_copy(gr.at[a], stg.at[s, pl.ds(h * NJ, NJ)], gsem.at[s]).start()

    fetch(0, 0)

    @pl.loop(0, NG // 2)
    def _(i):
        s = lax.rem(i, 2)

        @pl.when(i >= 2)
        def _():
            landed(ost.at[s], osem.at[s])

        @pl.when(i + 1 < NG // 2)
        def _():
            fetch(i + 1, 1 - s)

        landed(stx.at[s], xsem.at[s])
        landed(stg.at[s], gsem.at[s])
        xb = stx[s].reshape(2 * T, D)
        gb = stg[s].reshape(2 * T, D)
        gate_pre = dot(xb, wg[...])
        up_pre = dot(xb, wu[...])
        hgrad = dot(gb, wd[...], 1, 1)
        sigma = jax.nn.sigmoid(gate_pre)
        act = gate_pre * sigma
        hid = (act * up_pre).astype(BF)
        gg = (hgrad * up_pre * sigma * (1.0 + gate_pre * (1.0 - sigma))).astype(BF)
        ug = (hgrad * act).astype(BF)
        for h in range(2):
            a = group_from(grp, 2 * i + h)
            for n, (val, out) in enumerate(((hid, hid_o), (gg, gg_o), (ug, ug_o))):
                ost[s, h, n] = val[h * T : (h + 1) * T, :]
                pltpu.make_async_copy(ost.at[s, h, n], out.at[a], osem.at[s]).start()

    pos_o[...] = pos_r[...]
    for s in range(2):
        landed(ost.at[s], osem.at[s])
    for k in range(1, NJ):
        to = lax.rem(own + k, NJ)
        landed(rank_s.at[to], ms.at[k])
    for i in range(7):
        landed(x_hbm, axs.at[i])
    for d in range(1, NG):
        a = group_to(grp, d)
        landed(pos_s.at[a], ps.at[d])
        landed(s1.at[a], q1s.at[d])
        landed(pbuf.at[a], p2s.at[d])
    for a in range(NG):
        landed(s2.at[a, pl.ds(0, (NJ - 1) * CAP)], q2s.at[a])


def combine_kernel(
    c_ref, pos_ref, xr, gr, hid_hbm, gg_hbm, ug_hbm, wg_hbm, wu_hbm,
    gin_o, dg_o, du_o, dd_o,
    hid, gg, ug, wg, wu, dx, rr1, s2, rr2, xcol, gcol, ogu, od,
    lsem, t1s, t1r, t2s, t2r, xsem, gsem, gusem, dsem,
):
    grp, own = lax.axis_index("group"), lax.axis_index("expert")
    barrier = enter(grp, own)
    loads = [
        pltpu.make_async_copy(src, dst, lsem.at[n])
        for n, (src, dst) in enumerate(
            ((gg_hbm, gg), (ug_hbm, ug), (wg_hbm, wg), (wu_hbm, wu), (hid_hbm, hid))
        )
    ]
    for w in loads:
        w.start()
    for w in loads[:4]:
        w.wait()
    pl.semaphore_wait(barrier, NG + NJ - 2)

    @pl.loop(0, NG // 2)
    def _(i):
        tops = [group_to(grp, 2 * i + h) for h in range(2)]
        ggb = jnp.concatenate([gg[a] for a in tops], axis=0)
        ugb = jnp.concatenate([ug[a] for a in tops], axis=0)
        for c in range(0, D, 512):
            part = dot(ggb, wg[c : c + 512, :], 1, 1) + dot(ugb, wu[c : c + 512, :], 1, 1)
            part = part.astype(BF)
            for h in range(2):
                dx[tops[h], :, c : c + 512] = part[h * T : (h + 1) * T, :]
        for a in tops:
            for k in range(1, NJ):
                to = lax.rem(own + k, NJ)
                at = pl.ds(pl.multiple_of(to * CAP, CAP), CAP)
                back = pl.ds(pl.multiple_of(own * CAP, CAP), CAP)
                send(dx.at[a, at], rr1.at[a, back], t1s.at[a], t1r.at[a], (grp, to))
            at = pl.ds(pl.multiple_of(own * CAP, CAP), CAP)
            pltpu.make_async_copy(dx.at[a, at], rr1.at[a, at], t1r.at[a]).start()

    loads[4].wait()
    spot = iota((PG, T), 0)

    def fetch(c, s):
        at = pl.ds(pl.multiple_of(c * 256, 256), 256)
        pltpu.make_async_copy(xr.at[:, at], xcol.at[s], xsem.at[s]).start()
        pltpu.make_async_copy(gr.at[:, at], gcol.at[s], gsem.at[s]).start()

    fetch(0, 0)

    @pl.loop(0, NG // 2)
    def _(i):
        s = lax.rem(i, 2)

        @pl.when(i >= 2)
        def _():
            landed(ogu.at[s], gusem.at[s])
            landed(od.at[s], dsem.at[s])

        @pl.when(i + 1 < NG // 2)
        def _():
            fetch(i + 1, 1 - s)

        landed(xcol.at[s], xsem.at[s])
        landed(gcol.at[s], gsem.at[s])
        at = pl.ds(pl.multiple_of(i * 256, 256), 256)
        xc = xcol[s]
        ogu[s, 0] = dot(xc, gg[...].reshape(ROWS, FF), 0, 0).astype(BF)
        ogu[s, 1] = dot(xc, ug[...].reshape(ROWS, FF), 0, 0).astype(BF)
        od[s] = dot(hid[...].reshape(ROWS, FF), gcol[s], 0, 0).astype(BF)
        pltpu.make_async_copy(ogu.at[s, 0], dg_o.at[at, :], gusem.at[s]).start()
        pltpu.make_async_copy(ogu.at[s, 1], du_o.at[at, :], gusem.at[s]).start()
        pltpu.make_async_copy(od.at[s], dd_o.at[:, at], dsem.at[s]).start()

        for h in range(2):
            d = 2 * i + h
            a = group_to(grp, d)
            landed(rr1.at[a], t1r.at[a])
            hot = jnp.where(spot == pos_ref[a, 0:1, :], 1.0, 0.0).astype(BF)
            for c in range(0, D, 512):
                s2[a, :, c : c + 512] = dot(hot, rr1[a, :, c : c + 512]).astype(BF)

            if h == 0:
                @pl.when(d > 0)
                def _():
                    send(s2.at[a], rr2.at[grp], t2s.at[d], t2r.at[grp], (a, own))

                @pl.when(d == 0)
                def _():
                    pltpu.make_async_copy(s2.at[a], rr2.at[a], t2r.at[a]).start()
            else:
                send(s2.at[a], rr2.at[grp], t2s.at[d], t2r.at[grp], (a, own))

    for a in range(NG):
        landed(rr2.at[a], t2r.at[a])
    for c in range(0, D, 512):
        rows = rr2[:, :, c : c + 512].reshape(NG * PG, 512)
        gin_o[:, c : c + 512] = dot(c_ref[...], rows, 0, 0).astype(BF)

    for s in range(2):
        landed(ogu.at[s], gusem.at[s])
        landed(od.at[s], dsem.at[s])
    for a in range(NG):
        landed(dx.at[a, pl.ds(0, (NJ - 1) * CAP)], t1s.at[a])
    for d in range(1, NG):
        landed(s2.at[group_to(grp, d)], t2s.at[d])


def body(tokens_in, out_grad, expert_ids, gate_weights, w_gate, w_up, w_down):
    hbm = pl.BlockSpec(memory_space=pl.ANY)
    vm = pl.BlockSpec(memory_space=pltpu.VMEM)
    sem = pltpu.SemaphoreType.DMA
    shape = jax.ShapeDtypeStruct
    wg, wu, wd = w_gate[0], w_up[0], w_down[0]
    xr, gr, hid, gg, ug, hots, pos = pl.pallas_call(
        dispatch_kernel,
        name="dispatch",
        out_shape=(
            shape((NG, NJ, CAP, D), BF), shape((NG, NJ, CAP, D), BF),
            shape((NG, T, FF), BF), shape((NG, T, FF), BF), shape((NG, T, FF), BF),
            shape((NG * PG, T), BF), shape((NG, 8, 128), I32),
        ),
        in_specs=[vm, vm, hbm, vm, hbm, hbm, hbm],
        out_specs=(hbm, hbm, hbm, hbm, hbm, vm, vm),
        scratch_shapes=[
            pltpu.VMEM((NJ, T, D), BF),
            pltpu.VMEM((NG, NJ, CAP, D), BF),
            pltpu.VMEM((NG, PG, D), BF),
            pltpu.VMEM((NG, PG, D), BF),
            pltpu.VMEM((NG, NJ * CAP, D), BF),
            pltpu.VMEM((2, 2 * NJ, CAP, D), BF),
            pltpu.VMEM((2, 2 * NJ, CAP, D), BF),
            pltpu.VMEM((D, FF), BF), pltpu.VMEM((D, FF), BF), pltpu.VMEM((FF, D), BF),
            pltpu.VMEM((2, 2, 3, T, FF), BF),
            pltpu.VMEM((NJ, NG, T), I32), pltpu.VMEM((NJ, NG, T), I32),
            pltpu.VMEM((NG, 8, 128), I32), pltpu.VMEM((NG, 8, 128), I32),
            pltpu.VMEM((E, T), I32), pltpu.VMEM((E, T), F32),
            sem((7,)), sem((NJ,)), sem((NJ,)), sem((NJ,)),
            sem((NG,)), sem((NG,)), sem((NG,)), sem((NG,)), sem((NG,)), sem((NG,)),
            sem((NG,)), sem((NG,)), sem((3,)), sem((2,)), sem((2,)), sem((2,)),
        ],
        compiler_params=pltpu.CompilerParams(
            collective_id=0, has_side_effects=True, vmem_limit_bytes=VMEM_LIMIT
        ),
    )(expert_ids.T, gate_weights.T, tokens_in, out_grad, wg, wu, wd)
    grad_in, d_gate, d_up, d_down = pl.pallas_call(
        combine_kernel,
        name="combine",
        out_shape=(
            shape((T, D), BF), shape((D, FF), BF), shape((D, FF), BF), shape((FF, D), BF),
        ),
        in_specs=[vm, vm] + [hbm] * 7,
        out_specs=(vm, hbm, hbm, hbm),
        scratch_shapes=[
            pltpu.VMEM((NG, T, FF), BF), pltpu.VMEM((NG, T, FF), BF), pltpu.VMEM((NG, T, FF), BF),
            pltpu.VMEM((D, FF), BF), pltpu.VMEM((D, FF), BF),
            pltpu.VMEM((NG, T, D), BF),
            pltpu.VMEM((NG, T, D), BF),
            pltpu.VMEM((NG, PG, D), BF),
            pltpu.VMEM((NG, PG, D), BF),
            pltpu.VMEM((2, ROWS, 256), BF), pltpu.VMEM((2, ROWS, 256), BF),
            pltpu.VMEM((2, 2, 256, FF), BF), pltpu.VMEM((2, FF, 256), BF),
            sem((5,)), sem((NG,)), sem((NG,)), sem((NG,)), sem((NG,)),
            sem((2,)), sem((2,)), sem((2,)), sem((2,)),
        ],
        compiler_params=pltpu.CompilerParams(
            collective_id=1, has_side_effects=True, vmem_limit_bytes=VMEM_LIMIT
        ),
    )(hots, pos, xr.reshape(ROWS, D), gr.reshape(ROWS, D), hid, gg, ug, wg, wu)
    return grad_in, d_gate[None], d_up[None], d_down[None]


def solution(mesh):
    both = ("group", "expert")
    return jax.shard_map(
        body,
        mesh=mesh,
        in_specs=(P(both, None),) * 4 + (P(both, None, None),) * 3,
        out_specs=(P(both, None),) + (P(both, None, None),) * 3,
        check_vma=False,
    )
```

```python
import jax
import jax.numpy as jnp
from jax import lax
from jax.experimental import pallas as pl
from jax.experimental.pallas import tpu as pltpu
from jax.sharding import PartitionSpec as P

NG, NJ = 16, 8
T, D, FF = 128, 2048, 768
CAP = 16
PG = 64
E = NG * NJ
ROWS = NG * NJ * CAP
BF, F32, I32 = jnp.bfloat16, jnp.float32, jnp.int32
MESH = pl.DeviceIdType.MESH
VMEM_LIMIT = 67043328


def dot(a, b, ca=1, cb=0):
    return lax.dot_general(a, b, (((ca,), (cb,)), ((), ())), preferred_element_type=F32)


NEAR = ((0, 1), (1, 0), (0, 3), (3, 0))
DIAG = ((1, 1), (3, 3), (1, 3), (3, 1))
LONG = ((1, 2), (2, 1), (3, 2), (2, 3))
FAR = ((2, 2), (0, 2), (2, 0))
SETS = (NEAR, DIAG, LONG, FAR + ((0, 0),))
OUTWARD = FAR[:1] + LONG + FAR[1:] + DIAG + NEAR


def shift_of(d):
    if isinstance(d, tuple):
        return d
    if isinstance(d, int):
        return d % 4, (d // 4 + d % 4) % 4
    dy = lax.rem(d, 4)
    return dy, lax.rem(lax.div(d, 4) + dy, 4)


def group_to(grp, d):
    dy, dx = shift_of(d)
    return lax.rem(lax.div(grp, 4) + dy, 4) * 4 + lax.rem(lax.rem(grp, 4) + dx, 4)


def group_from(grp, d):
    dy, dx = shift_of(d)
    return lax.rem(lax.div(grp, 4) - dy + 4, 4) * 4 + lax.rem(lax.rem(grp, 4) - dx + 4, 4)


def enter(grp, own):
    barrier = pltpu.get_barrier_semaphore()
    for d in range(1, NG):
        pl.semaphore_signal(barrier, inc=1, device_id=(group_to(grp, d), own), device_id_type=MESH)
    for k in range(1, NJ):
        pl.semaphore_signal(
            barrier, inc=1, device_id=(grp, lax.rem(own + k, NJ)), device_id_type=MESH
        )
    return barrier


def send(src, dst, ssem, rsem, device):
    pltpu.make_async_remote_copy(
        src_ref=src, dst_ref=dst, send_sem=ssem, recv_sem=rsem,
        device_id=device, device_id_type=MESH,
    ).start()


def landed(ref, sem):
    pltpu.make_async_copy(ref, ref, sem).wait()


def iota(shape, dim):
    return lax.broadcasted_iota(I32, shape, dim)


def dispatch_kernel(
    ids_ref, gw_ref, x_hbm, g_ref, wg_hbm, wu_hbm, wd_hbm,
    xr, gr, hid_o, gg_o, ug_o, c_o, pos_o,
    ax, pbuf, s1, r1, s2, stx, stg, wg, wu, wd, ost,
    rank_s, rank_r, pos_s, pos_r, post, wt,
    axs, axr, ms, mr, ps, pr, q1s, q1r, q2s, q2r, p2s, p2r, wsem, xsem, gsem, osem,
):
    grp, own = lax.axis_index("group"), lax.axis_index("expert")
    partner = own + 1 - 2 * lax.rem(own, 2)
    barrier = enter(grp, own)
    loads = [
        pltpu.make_async_copy(wg_hbm, wg, wsem.at[0]),
        pltpu.make_async_copy(wu_hbm, wu, wsem.at[1]),
        pltpu.make_async_copy(wd_hbm, wd, wsem.at[2]),
    ]
    pltpu.make_async_copy(x_hbm, ax.at[own], axr.at[own]).start()

    row, lane = iota((E, T), 0), iota((E, T), 1)
    before = jnp.where(row < lane, 1.0, 0.0).astype(BF)
    named = jnp.zeros((E, T), F32)
    weight = jnp.zeros((E, T), F32)
    named_p = jnp.zeros((E, T), F32)
    row_p = lax.rem(row, NG) * NJ + lax.div(row, NG)
    for k in range(8):
        idk = ids_ref[k : k + 1, :]
        gwk = gw_ref[k : k + 1, :]
        named = jnp.where(row == idk, 1.0, named)
        weight = jnp.where(row == idk, gwk, weight)
        named_p = jnp.where(row_p == idk, 1.0, named_p)
    rank = dot(named.astype(BF), before)
    rank_p = dot(named_p.astype(BF), before)
    counts = dot(named.astype(BF), jnp.ones((T, T), BF))
    ahead = jnp.where(
        (lax.div(row, NJ) == lax.div(lane, NJ)) & (lane < row), 1.0, 0.0
    ).astype(BF)
    starts = dot(ahead, counts.astype(BF))
    post[...] = jnp.where(named > 0.5, starts + rank, -1.0).astype(I32)
    wt[...] = weight
    rank_s[...] = jnp.where(named_p > 0.5, rank_p, -1.0).astype(I32).reshape(NJ, NG, T)
    mine = lax.rem(row, NJ) == lax.div(lane, CAP)
    pick = jnp.where(lax.div(iota((NG, E), 1), NJ) == iota((NG, E), 0), 1.0, 0.0).astype(BF)
    start_row = dot(pick, jnp.where(mine, starts, 0.0).astype(BF))
    count_row = dot(pick, jnp.where(mine, counts, 0.0).astype(BF))
    slot = lax.rem(iota((NG, E), 1), CAP).astype(F32)
    pos = jnp.where(slot < count_row, start_row + slot, -1.0).astype(I32)
    for a in range(NG):
        pos_s[a] = jnp.broadcast_to(pos[a : a + 1, :], (8, 128))
    rank_r[own] = rank_s[own]
    pos_r[grp] = pos_s[grp]

    pl.semaphore_wait(barrier, NG + NJ - 2)

    for k in range(1, NJ):
        to = lax.rem(own + k, NJ)
        send(rank_s.at[to], rank_r.at[own], ms.at[k], mr.at[own], (grp, to))
    for i in range(1, 4):
        to = lax.rem(own + 2 * i, NJ)
        send(x_hbm, ax.at[own], axs.at[i], axr.at[own], (grp, to))
    send(x_hbm, ax.at[own], axs.at[0], axr.at[own], (grp, partner))

    spot = iota((PG, T), 0)
    for steps in SETS:
        picks, scales = [], []
        for d in steps:
            a = group_to(grp, d)
            at = pl.ds(pl.multiple_of(a * NJ, NJ), NJ)
            prow, wrow = post[at, :], wt[at, :]
            hot = jnp.zeros((PG, T), F32)
            wsel = jnp.zeros((PG, T), F32)
            for e in range(NJ):
                hit = spot == prow[e : e + 1, :]
                hot = jnp.where(hit, 1.0, hot)
                wsel = jnp.where(hit, wrow[e : e + 1, :], wsel)
            c_o[pl.ds(pl.multiple_of(a * PG, PG), PG), :] = hot.astype(BF)
            picks.append(hot.astype(BF))
            scales.append(jnp.sum(wsel, axis=1, keepdims=True))
        hots = jnp.concatenate(picks, axis=0)
        scale = jnp.concatenate(scales, axis=0)
        for c in range(0, D, 512):
            part = (scale * dot(hots, g_ref[:, c : c + 512])).astype(BF)
            for q, d in enumerate(steps):
                s1[group_to(grp, d), :, c : c + 512] = part[q * PG : (q + 1) * PG, :]
        ends = [d for d in steps if d != (0, 0)]
        for d in ends:
            a = group_to(grp, d)
            send(pos_s.at[a], pos_r.at[grp], ps.at[a], pr.at[grp], (a, own))
        for r in range(0, PG, 16):
            for d in ends:
                a = group_to(grp, d)
                send(s1.at[a, pl.ds(r, 16)], r1.at[grp, pl.ds(r, 16)],
                     q1s.at[a], q1r.at[grp], (a, own))
    for w in loads:
        w.start()

    def spread(a, rows_ref):
        hot = jnp.where(spot == pos_r[a, 0:1, :], 1.0, 0.0).astype(BF)
        for c in range(0, D, 512):
            s2[a, :, c : c + 512] = dot(hot, rows_ref[a, :, c : c + 512], 0, 0).astype(BF)
        for k in range(1, NJ):
            to = lax.rem(own + k, NJ)
            at = pl.ds(pl.multiple_of(to * CAP, CAP), CAP)
            send(s2.at[a, at], gr.at[own, a], q2s.at[a], q2r.at[own], (grp, to))
        at = pl.ds(pl.multiple_of(own * CAP, CAP), CAP)
        pltpu.make_async_copy(s2.at[a, at], gr.at[own, a], q2r.at[own]).start()

    spread(grp, s1)

    for k in range(1, NJ):
        frm = lax.rem(own + k, NJ)
        landed(rank_r.at[frm], mr.at[frm])

    cap_row = iota((CAP, T), 0)

    def source(n):
        side = lax.rem(n, 2)
        return lax.rem(own + (partner - own) * side - (n - side) + NJ, NJ)

    @pl.loop(0, NJ)
    def _(n):
        j = source(n)
        landed(ax.at[j], axr.at[j])

        @pl.when((n >= 2) & (lax.rem(n, 2) == 0))
        def _():
            send(ax.at[j], ax.at[j], axs.at[3 + lax.div(n, 2)], axr.at[j], (grp, partner))

        hots = jnp.concatenate(
            [
                jnp.where(cap_row == rank_r[j, a : a + 1, :], 1.0, 0.0).astype(BF)
                for a in range(NG)
            ],
            axis=0,
        )
        for c in range(0, D, 512):
            part = dot(hots, ax[j, :, c : c + 512]).astype(BF)
            pbuf[j, :, :, c : c + 512] = part.reshape(NG, CAP, 512)
        for d in OUTWARD:
            a = group_to(grp, d)
            send(pbuf.at[j, a], xr.at[j, grp], p2s.at[j], p2r.at[j], (a, own))
        pltpu.make_async_copy(pbuf.at[j, grp], xr.at[j, grp], p2r.at[j]).start()

    for steps in SETS:
        for d in steps:
            if d != (0, 0):
                a = group_from(grp, d)
                landed(pos_r.at[a], pr.at[a])
                landed(r1.at[a], q1r.at[a])
                spread(a, r1)

    for w in loads:
        w.wait()

    def fetch(n, s):
        j = source(n)
        landed(xr.at[j], p2r.at[j])
        landed(gr.at[j], q2r.at[j])
        pltpu.make_async_copy(xr.at[j], stx.at[s], xsem.at[s]).start()
        pltpu.make_async_copy(gr.at[j], stg.at[s], gsem.at[s]).start()

    @pl.loop(0, NJ)
    def _(n):
        s = lax.rem(n, 2)

        @pl.when(n >= 2)
        def _():
            landed(ost.at[s], osem.at[s])

        fetch(n, s)
        landed(stx.at[s], xsem.at[s])
        landed(stg.at[s], gsem.at[s])
        xb = stx[s].reshape(2 * T, D)
        gb = stg[s].reshape(2 * T, D)
        gate_pre = dot(xb, wg[...])
        up_pre = dot(xb, wu[...])
        hgrad = dot(gb, wd[...], 1, 1)
        sigma = jax.nn.sigmoid(gate_pre)
        act = gate_pre * sigma
        ost[s, 0] = (act * up_pre).astype(BF)
        ost[s, 1] = (hgrad * up_pre * sigma * (1.0 + gate_pre * (1.0 - sigma))).astype(BF)
        ost[s, 2] = (hgrad * act).astype(BF)
        for v, out in enumerate((hid_o, gg_o, ug_o)):
            pltpu.make_async_copy(ost.at[s, v], out.at[source(n)], osem.at[s]).start()

    pos_o[...] = pos_r[...]
    for s in range(2):
        landed(ost.at[s], osem.at[s])
    for k in range(1, NJ):
        to = lax.rem(own + k, NJ)
        landed(rank_s.at[to], ms.at[k])
    for i in range(7):
        landed(x_hbm, axs.at[i])
    for d in range(1, NG):
        a = group_to(grp, d)
        landed(pos_s.at[a], ps.at[a])
        landed(s1.at[a], q1s.at[a])
    for j in range(NJ):
        landed(pbuf.at[j, pl.ds(0, NG - 1)], p2s.at[j])
    for a in range(NG):
        landed(s2.at[a, pl.ds(0, (NJ - 1) * CAP)], q2s.at[a])


def combine_kernel(
    c_ref, pos_ref, xr, gr, hid_hbm, gg_hbm, ug_hbm, wg_hbm, wu_hbm,
    gin_o, dg_o, du_o, dd_o,
    hid, gg, ug, wg, wu, dx, rr1, s2, rr2, xcol, gcol, ogu, od,
    lsem, t1s, t1r, t2s, t2r, xsem, gsem, gusem, dsem,
):
    grp, own = lax.axis_index("group"), lax.axis_index("expert")
    barrier = enter(grp, own)
    loads = [
        pltpu.make_async_copy(src, dst, lsem.at[n])
        for n, (src, dst) in enumerate(
            ((gg_hbm, gg), (ug_hbm, ug), (wg_hbm, wg), (wu_hbm, wu), (hid_hbm, hid))
        )
    ]
    for w in loads:
        w.start()
    for w in loads[:4]:
        w.wait()
    pl.semaphore_wait(barrier, NG + NJ - 2)

    @pl.loop(0, NG // 2)
    def _(i):
        tops = [group_to(grp, 2 * i + h) for h in range(2)]
        ats = [pl.ds(pl.multiple_of(a * CAP, CAP), CAP) for a in tops]
        ggb = jnp.concatenate([gg[j, at, :] for at in ats for j in range(NJ)], axis=0)
        ugb = jnp.concatenate([ug[j, at, :] for at in ats for j in range(NJ)], axis=0)
        for c in range(0, D, 512):
            part = dot(ggb, wg[c : c + 512, :], 1, 1) + dot(ugb, wu[c : c + 512, :], 1, 1)
            part = part.astype(BF)
            for h in range(2):
                dx[tops[h], :, c : c + 512] = part[h * T : (h + 1) * T, :]
        for a in tops:
            for k in range(1, NJ):
                to = lax.rem(own + k, NJ)
                at = pl.ds(pl.multiple_of(to * CAP, CAP), CAP)
                back = pl.ds(pl.multiple_of(own * CAP, CAP), CAP)
                send(dx.at[a, at], rr1.at[a, back], t1s.at[a], t1r.at[a], (grp, to))
            at = pl.ds(pl.multiple_of(own * CAP, CAP), CAP)
            pltpu.make_async_copy(dx.at[a, at], rr1.at[a, at], t1r.at[a]).start()

    loads[4].wait()
    spot = iota((PG, T), 0)

    def fetch(c, s):
        at = pl.ds(pl.multiple_of(c * 256, 256), 256)
        pltpu.make_async_copy(xr.at[:, at], xcol.at[s], xsem.at[s]).start()
        pltpu.make_async_copy(gr.at[:, at], gcol.at[s], gsem.at[s]).start()

    fetch(0, 0)

    @pl.loop(0, NG // 2)
    def _(i):
        s = lax.rem(i, 2)

        @pl.when(i >= 2)
        def _():
            landed(ogu.at[s], gusem.at[s])
            landed(od.at[s], dsem.at[s])

        @pl.when(i + 1 < NG // 2)
        def _():
            fetch(i + 1, 1 - s)

        landed(xcol.at[s], xsem.at[s])
        landed(gcol.at[s], gsem.at[s])
        at = pl.ds(pl.multiple_of(i * 256, 256), 256)
        xc = xcol[s]
        ogu[s, 0] = dot(xc, gg[...].reshape(ROWS, FF), 0, 0).astype(BF)
        ogu[s, 1] = dot(xc, ug[...].reshape(ROWS, FF), 0, 0).astype(BF)
        od[s] = dot(hid[...].reshape(ROWS, FF), gcol[s], 0, 0).astype(BF)
        pltpu.make_async_copy(ogu.at[s, 0], dg_o.at[at, :], gusem.at[s]).start()
        pltpu.make_async_copy(ogu.at[s, 1], du_o.at[at, :], gusem.at[s]).start()
        pltpu.make_async_copy(od.at[s], dd_o.at[:, at], dsem.at[s]).start()

        for h in range(2):
            d = 2 * i + h
            a = group_to(grp, d)
            landed(rr1.at[a], t1r.at[a])
            hot = jnp.where(spot == pos_ref[a, 0:1, :], 1.0, 0.0).astype(BF)
            for c in range(0, D, 512):
                s2[a, :, c : c + 512] = dot(hot, rr1[a, :, c : c + 512]).astype(BF)

            if h == 0:
                @pl.when(d > 0)
                def _():
                    send(s2.at[a], rr2.at[grp], t2s.at[d], t2r.at[grp], (a, own))

                @pl.when(d == 0)
                def _():
                    pltpu.make_async_copy(s2.at[a], rr2.at[a], t2r.at[a]).start()
            else:
                send(s2.at[a], rr2.at[grp], t2s.at[d], t2r.at[grp], (a, own))

    for a in range(NG):
        landed(rr2.at[a], t2r.at[a])
    for c in range(0, D, 512):
        rows = rr2[:, :, c : c + 512].reshape(NG * PG, 512)
        gin_o[:, c : c + 512] = dot(c_ref[...], rows, 0, 0).astype(BF)

    for s in range(2):
        landed(ogu.at[s], gusem.at[s])
        landed(od.at[s], dsem.at[s])
    for a in range(NG):
        landed(dx.at[a, pl.ds(0, (NJ - 1) * CAP)], t1s.at[a])
    for d in range(1, NG):
        landed(s2.at[group_to(grp, d)], t2s.at[d])


def body(tokens_in, out_grad, expert_ids, gate_weights, w_gate, w_up, w_down):
    hbm = pl.BlockSpec(memory_space=pl.ANY)
    vm = pl.BlockSpec(memory_space=pltpu.VMEM)
    sem = pltpu.SemaphoreType.DMA
    shape = jax.ShapeDtypeStruct
    wg, wu, wd = w_gate[0], w_up[0], w_down[0]
    xr, gr, hid, gg, ug, hots, pos = pl.pallas_call(
        dispatch_kernel,
        name="dispatch",
        out_shape=(
            shape((NJ, NG, CAP, D), BF), shape((NJ, NG, CAP, D), BF),
            shape((NJ, 2 * T, FF), BF), shape((NJ, 2 * T, FF), BF), shape((NJ, 2 * T, FF), BF),
            shape((NG * PG, T), BF), shape((NG, 8, 128), I32),
        ),
        in_specs=[vm, vm, hbm, vm, hbm, hbm, hbm],
        out_specs=(hbm, hbm, hbm, hbm, hbm, vm, vm),
        scratch_shapes=[
            pltpu.VMEM((NJ, T, D), BF),
            pltpu.VMEM((NJ, NG, CAP, D), BF),
            pltpu.VMEM((NG, PG, D), BF),
            pltpu.VMEM((NG, PG, D), BF),
            pltpu.VMEM((NG, NJ * CAP, D), BF),
            pltpu.VMEM((2, NG, CAP, D), BF),
            pltpu.VMEM((2, NG, CAP, D), BF),
            pltpu.VMEM((D, FF), BF), pltpu.VMEM((D, FF), BF), pltpu.VMEM((FF, D), BF),
            pltpu.VMEM((2, 3, 2 * T, FF), BF),
            pltpu.VMEM((NJ, NG, T), I32), pltpu.VMEM((NJ, NG, T), I32),
            pltpu.VMEM((NG, 8, 128), I32), pltpu.VMEM((NG, 8, 128), I32),
            pltpu.VMEM((E, T), I32), pltpu.VMEM((E, T), F32),
            sem((7,)), sem((NJ,)), sem((NJ,)), sem((NJ,)),
            sem((NG,)), sem((NG,)), sem((NG,)), sem((NG,)), sem((NG,)), sem((NG,)),
            sem((NG,)), sem((NG,)), sem((3,)), sem((2,)), sem((2,)), sem((2,)),
        ],
        compiler_params=pltpu.CompilerParams(
            collective_id=0, has_side_effects=True, vmem_limit_bytes=VMEM_LIMIT
        ),
    )(expert_ids.T, gate_weights.T, tokens_in, out_grad, wg, wu, wd)
    grad_in, d_gate, d_up, d_down = pl.pallas_call(
        combine_kernel,
        name="combine",
        out_shape=(
            shape((T, D), BF), shape((D, FF), BF), shape((D, FF), BF), shape((FF, D), BF),
        ),
        in_specs=[vm, vm] + [hbm] * 7,
        out_specs=(vm, hbm, hbm, hbm),
        scratch_shapes=[
            pltpu.VMEM((NJ, 2 * T, FF), BF), pltpu.VMEM((NJ, 2 * T, FF), BF),
            pltpu.VMEM((NJ, 2 * T, FF), BF),
            pltpu.VMEM((D, FF), BF), pltpu.VMEM((D, FF), BF),
            pltpu.VMEM((NG, T, D), BF),
            pltpu.VMEM((NG, T, D), BF),
            pltpu.VMEM((NG, PG, D), BF),
            pltpu.VMEM((NG, PG, D), BF),
            pltpu.VMEM((2, ROWS, 256), BF), pltpu.VMEM((2, ROWS, 256), BF),
            pltpu.VMEM((2, 2, 256, FF), BF), pltpu.VMEM((2, FF, 256), BF),
            sem((5,)), sem((NG,)), sem((NG,)), sem((NG,)), sem((NG,)),
            sem((2,)), sem((2,)), sem((2,)), sem((2,)),
        ],
        compiler_params=pltpu.CompilerParams(
            collective_id=1, has_side_effects=True, vmem_limit_bytes=VMEM_LIMIT
        ),
    )(hots, pos, xr.reshape(ROWS, D), gr.reshape(ROWS, D), hid, gg, ug, wg, wu)
    return grad_in, d_gate[None], d_up[None], d_down[None]


def solution(mesh):
    both = ("group", "expert")
    return jax.shard_map(
        body,
        mesh=mesh,
        in_specs=(P(both, None),) * 4 + (P(both, None, None),) * 3,
        out_specs=(P(both, None),) + (P(both, None, None),) * 3,
        check_vma=False,
    )
```

```python
import jax
import jax.numpy as jnp
from jax import lax
from jax.experimental import pallas as pl
from jax.experimental.pallas import tpu as pltpu
from jax.sharding import PartitionSpec as P

NG, NJ = 16, 8
T, D, FF = 128, 2048, 768
CAP = 16
PG = 64
E = NG * NJ
DP = 1024
ROWS = NG * NJ * CAP
BF, F32, I32 = jnp.bfloat16, jnp.float32, jnp.int32
MESH = pl.DeviceIdType.MESH
VMEM_LIMIT = 67043328


def dot(a, b, ca=1, cb=0):
    return lax.dot_general(a, b, (((ca,), (cb,)), ((), ())), preferred_element_type=F32)


NEAR = ((0, 1), (1, 0), (0, 3), (3, 0))
DIAG = ((1, 1), (3, 3), (1, 3), (3, 1))
LONG = ((1, 2), (2, 1), (3, 2), (2, 3))
FAR = ((2, 2), (0, 2), (2, 0))
SETS = (NEAR, DIAG, LONG, FAR + ((0, 0),))
OUTWARD = FAR[:1] + LONG + FAR[1:] + DIAG + NEAR


def shift_of(d):
    if isinstance(d, tuple):
        return d
    if isinstance(d, int):
        return d % 4, (d // 4 + d % 4) % 4
    dy = lax.rem(d, 4)
    return dy, lax.rem(lax.div(d, 4) + dy, 4)


def group_to(grp, d):
    dy, dx = shift_of(d)
    return lax.rem(lax.div(grp, 4) + dy, 4) * 4 + lax.rem(lax.rem(grp, 4) + dx, 4)


def group_from(grp, d):
    dy, dx = shift_of(d)
    return lax.rem(lax.div(grp, 4) - dy + 4, 4) * 4 + lax.rem(lax.rem(grp, 4) - dx + 4, 4)


def enter(grp, own):
    barrier = pltpu.get_barrier_semaphore()
    for d in range(1, NG):
        pl.semaphore_signal(barrier, inc=1, device_id=(group_to(grp, d), own), device_id_type=MESH)
    for k in range(1, NJ):
        pl.semaphore_signal(
            barrier, inc=1, device_id=(grp, lax.rem(own + k, NJ)), device_id_type=MESH
        )
    return barrier


def send(src, dst, ssem, rsem, device):
    pltpu.make_async_remote_copy(
        src_ref=src, dst_ref=dst, send_sem=ssem, recv_sem=rsem,
        device_id=device, device_id_type=MESH,
    ).start()


def landed(ref, sem):
    pltpu.make_async_copy(ref, ref, sem).wait()


def iota(shape, dim):
    return lax.broadcasted_iota(I32, shape, dim)


def slots_of(rank_ref, j):
    spot = iota((CAP, T), 0)
    return jnp.concatenate(
        [jnp.where(spot == rank_ref[j, a : a + 1, :], 1.0, 0.0).astype(BF) for a in range(NG)],
        axis=0,
    )


def dispatch_kernel(
    ids_ref, gw_ref, x_hbm, g_ref, wg_hbm, wu_hbm, wd_hbm,
    xr, gr, hid_o, gg_o, ug_o, c_o, pos_o, rank_o,
    ax, pbuf, s1, r1, s2, stx, stg, wg, wu, wd, ost,
    rank_s, rank_r, pos_s, pos_r, post, wt,
    axs, axr, ms, mr, ps, pr, q1s, q1r, q2s, q2r, p2s, p2r, wsem, xsem, gsem, osem,
):
    grp, own = lax.axis_index("group"), lax.axis_index("expert")
    partner = own + 1 - 2 * lax.rem(own, 2)
    barrier = enter(grp, own)
    loads = [
        pltpu.make_async_copy(wg_hbm, wg, wsem.at[0]),
        pltpu.make_async_copy(wu_hbm, wu, wsem.at[1]),
        pltpu.make_async_copy(wd_hbm, wd, wsem.at[2]),
    ]
    pltpu.make_async_copy(x_hbm, ax.at[own], axr.at[own]).start()

    row, lane = iota((E, T), 0), iota((E, T), 1)
    before = jnp.where(row < lane, 1.0, 0.0).astype(BF)
    named = jnp.zeros((E, T), F32)
    weight = jnp.zeros((E, T), F32)
    named_p = jnp.zeros((E, T), F32)
    row_p = lax.rem(row, NG) * NJ + lax.div(row, NG)
    for k in range(8):
        idk = ids_ref[k : k + 1, :]
        gwk = gw_ref[k : k + 1, :]
        named = jnp.where(row == idk, 1.0, named)
        weight = jnp.where(row == idk, gwk, weight)
        named_p = jnp.where(row_p == idk, 1.0, named_p)
    rank = dot(named.astype(BF), before)
    rank_p = dot(named_p.astype(BF), before)
    counts = dot(named.astype(BF), jnp.ones((T, T), BF))
    ahead = jnp.where(
        (lax.div(row, NJ) == lax.div(lane, NJ)) & (lane < row), 1.0, 0.0
    ).astype(BF)
    starts = dot(ahead, counts.astype(BF))
    post[...] = jnp.where(named > 0.5, starts + rank, -1.0).astype(I32)
    wt[...] = weight
    rank_s[...] = jnp.where(named_p > 0.5, rank_p, -1.0).astype(I32).reshape(NJ, NG, T)
    mine = lax.rem(row, NJ) == lax.div(lane, CAP)
    pick = jnp.where(lax.div(iota((NG, E), 1), NJ) == iota((NG, E), 0), 1.0, 0.0).astype(BF)
    start_row = dot(pick, jnp.where(mine, starts, 0.0).astype(BF))
    count_row = dot(pick, jnp.where(mine, counts, 0.0).astype(BF))
    slot = lax.rem(iota((NG, E), 1), CAP).astype(F32)
    pos = jnp.where(slot < count_row, start_row + slot, -1.0).astype(I32)
    for a in range(NG):
        pos_s[a] = jnp.broadcast_to(pos[a : a + 1, :], (8, 128))
    rank_r[own] = rank_s[own]
    pos_r[grp] = pos_s[grp]

    pl.semaphore_wait(barrier, NG + NJ - 2)

    for k in range(1, NJ):
        to = lax.rem(own + k, NJ)
        send(rank_s.at[to], rank_r.at[own], ms.at[k], mr.at[own], (grp, to))
    for i in range(1, 4):
        to = lax.rem(own + 2 * i, NJ)
        send(x_hbm, ax.at[own], axs.at[i], axr.at[own], (grp, to))
    send(x_hbm, ax.at[own], axs.at[0], axr.at[own], (grp, partner))

    spot = iota((PG, T), 0)
    for steps in SETS:
        picks, scales = [], []
        for d in steps:
            a = group_to(grp, d)
            at = pl.ds(pl.multiple_of(a * NJ, NJ), NJ)
            prow, wrow = post[at, :], wt[at, :]
            hot = jnp.zeros((PG, T), F32)
            wsel = jnp.zeros((PG, T), F32)
            for e in range(NJ):
                hit = spot == prow[e : e + 1, :]
                hot = jnp.where(hit, 1.0, hot)
                wsel = jnp.where(hit, wrow[e : e + 1, :], wsel)
            c_o[pl.ds(pl.multiple_of(a * PG, PG), PG), :] = hot.astype(BF)
            picks.append(hot.astype(BF))
            scales.append(jnp.sum(wsel, axis=1, keepdims=True))
        hots = jnp.concatenate(picks, axis=0)
        scale = jnp.concatenate(scales, axis=0)
        for c in range(0, D, 512):
            part = (scale * dot(hots, g_ref[:, c : c + 512])).astype(BF)
            for q, d in enumerate(steps):
                s1[group_to(grp, d), :, c : c + 512] = part[q * PG : (q + 1) * PG, :]
        ends = [d for d in steps if d != (0, 0)]
        for d in ends:
            a = group_to(grp, d)
            send(pos_s.at[a], pos_r.at[grp], ps.at[a], pr.at[grp], (a, own))
        for r in range(0, PG, 16):
            for d in ends:
                a = group_to(grp, d)
                send(s1.at[a, pl.ds(r, 16)], r1.at[grp, pl.ds(r, 16)],
                     q1s.at[a], q1r.at[grp], (a, own))
    for w in loads:
        w.start()

    def spread(a, rows_ref):
        hot = jnp.where(spot == pos_r[a, 0:1, :], 1.0, 0.0).astype(BF)
        for c in range(0, D, 512):
            s2[a, :, c : c + 512] = dot(hot, rows_ref[a, :, c : c + 512], 0, 0).astype(BF)
        for k in range(1, NJ):
            to = lax.rem(own + k, NJ)
            at = pl.ds(pl.multiple_of(to * CAP, CAP), CAP)
            send(s2.at[a, at], gr.at[own, a], q2s.at[a], q2r.at[own], (grp, to))
        at = pl.ds(pl.multiple_of(own * CAP, CAP), CAP)
        pltpu.make_async_copy(s2.at[a, at], gr.at[own, a], q2r.at[own]).start()

    spread(grp, s1)

    for k in range(1, NJ):
        frm = lax.rem(own + k, NJ)
        landed(rank_r.at[frm], mr.at[frm])

    def source(n):
        side = lax.rem(n, 2)
        return lax.rem(own + (partner - own) * side - (n - side) + NJ, NJ)

    @pl.loop(0, NJ)
    def _(n):
        j = source(n)
        landed(ax.at[j], axr.at[j])

        @pl.when((n >= 2) & (lax.rem(n, 2) == 0))
        def _():
            send(ax.at[j], ax.at[j], axs.at[3 + lax.div(n, 2)], axr.at[j], (grp, partner))

        hots = slots_of(rank_r, j)
        for c in range(0, D, 512):
            part = dot(hots, ax[j, :, c : c + 512]).astype(BF)
            pbuf[j, :, :, c : c + 512] = part.reshape(NG, CAP, 512)
        for d in OUTWARD:
            a = group_to(grp, d)
            send(pbuf.at[j, a], xr.at[j, grp], p2s.at[j], p2r.at[j], (a, own))
        pltpu.make_async_copy(pbuf.at[j, grp], xr.at[j, grp], p2r.at[j]).start()

    for steps in SETS:
        for d in steps:
            if d != (0, 0):
                a = group_from(grp, d)
                landed(pos_r.at[a], pr.at[a])
                landed(r1.at[a], q1r.at[a])
                spread(a, r1)

    for w in loads:
        w.wait()

    def fetch(n, s):
        j = source(n)
        landed(xr.at[j], p2r.at[j])
        landed(gr.at[j], q2r.at[j])
        pltpu.make_async_copy(xr.at[j], stx.at[s], xsem.at[s]).start()
        pltpu.make_async_copy(gr.at[j], stg.at[s], gsem.at[s]).start()

    @pl.loop(0, NJ)
    def _(n):
        s = lax.rem(n, 2)

        @pl.when(n >= 2)
        def _():
            landed(ost.at[s], osem.at[s])

        fetch(n, s)
        landed(stx.at[s], xsem.at[s])
        landed(stg.at[s], gsem.at[s])
        xb = stx[s].reshape(2 * T, D)
        gb = stg[s].reshape(2 * T, D)
        gate_pre = dot(xb, wg[...])
        up_pre = dot(xb, wu[...])
        hgrad = dot(gb, wd[...], 1, 1)
        sigma = jax.nn.sigmoid(gate_pre)
        act = gate_pre * sigma
        ost[s, 0] = (act * up_pre).astype(BF)
        ost[s, 1] = (hgrad * up_pre * sigma * (1.0 + gate_pre * (1.0 - sigma))).astype(BF)
        ost[s, 2] = (hgrad * act).astype(BF)
        for v, out in enumerate((hid_o, gg_o, ug_o)):
            pltpu.make_async_copy(ost.at[s, v], out.at[source(n)], osem.at[s]).start()

    pos_o[...] = pos_r[...]
    rank_o[...] = rank_r[...]
    for s in range(2):
        landed(ost.at[s], osem.at[s])
    for k in range(1, NJ):
        to = lax.rem(own + k, NJ)
        landed(rank_s.at[to], ms.at[k])
    for i in range(7):
        landed(x_hbm, axs.at[i])
    for d in range(1, NG):
        a = group_to(grp, d)
        landed(pos_s.at[a], ps.at[a])
        landed(s1.at[a], q1s.at[a])
    for j in range(NJ):
        landed(pbuf.at[j, pl.ds(0, NG - 1)], p2s.at[j])
    for a in range(NG):
        landed(s2.at[a, pl.ds(0, (NJ - 1) * CAP)], q2s.at[a])


def combine_kernel(
    c_ref, pos_ref, rank_ref, xr, gr, hid_hbm, gg_hbm, ug_hbm, wg_hbm, wu_hbm,
    gin_o, dg_o, du_o, dd_o,
    hid, gg, ug, wg, wu, dxp, dxq, rrp, rrq, part, rrz, s2, rr2, xcol, gcol, ogu, od,
    lsem, p1s, p1r, p2s, p2r, t1s, t1r, t2s, t2r, xsem, gsem, gusem, dsem,
):
    grp, own = lax.axis_index("group"), lax.axis_index("expert")
    barrier = enter(grp, own)
    loads = [
        pltpu.make_async_copy(src, dst, lsem.at[n])
        for n, (src, dst) in enumerate(
            ((gg_hbm, gg), (ug_hbm, ug), (wg_hbm, wg), (wu_hbm, wu), (hid_hbm, hid))
        )
    ]
    for w in loads:
        w.start()
    for w in loads[:4]:
        w.wait()
    pl.semaphore_wait(barrier, NG + NJ - 2)

    def slot_rows(a):
        return pl.ds(pl.multiple_of(a * CAP, CAP), CAP)

    def input_rows(ggb, ugb, c):
        return (
            dot(ggb, wg[c : c + 512, :], 1, 1) + dot(ugb, wu[c : c + 512, :], 1, 1)
        ).astype(BF)

    @pl.loop(0, NJ)
    def _(n):
        j = lax.rem(own + 4 + n, NJ)
        for c in range(0, DP, 512):
            dxp[j, :, c : c + 512] = input_rows(gg[j], ug[j], c)
        for d in OUTWARD:
            a = group_to(grp, d)
            send(dxp.at[j, slot_rows(a)], rrp.at[j, slot_rows(grp)],
                 p1s.at[j], p1r.at[j], (a, own))
        pltpu.make_async_copy(
            dxp.at[j, slot_rows(grp)], rrp.at[j, slot_rows(grp)], p1r.at[j]
        ).start()

        tops = [group_to(grp, 2 * n + h) for h in range(2)]
        ats = [slot_rows(a) for a in tops]
        ggb = jnp.concatenate([gg[q, at, :] for at in ats for q in range(NJ)], axis=0)
        ugb = jnp.concatenate([ug[q, at, :] for at in ats for q in range(NJ)], axis=0)
        for c in range(DP, D, 512):
            rows = input_rows(ggb, ugb, c)
            for h in range(2):
                dxq[tops[h], :, c - DP : c - DP + 512] = rows[h * T : (h + 1) * T, :]
        for a in tops:
            for k in range(1, NJ):
                to = lax.rem(own + k, NJ)
                send(dxq.at[a, slot_rows(to)], rrq.at[a, slot_rows(own)],
                     t1s.at[a], t1r.at[a], (grp, to))
            pltpu.make_async_copy(
                dxq.at[a, slot_rows(own)], rrq.at[a, slot_rows(own)], t1r.at[a]
            ).start()

    loads[4].wait()
    spot = iota((PG, T), 0)

    def fetch(c, s):
        at = pl.ds(pl.multiple_of(c * 256, 256), 256)
        pltpu.make_async_copy(xr.at[:, at], xcol.at[s], xsem.at[s]).start()
        pltpu.make_async_copy(gr.at[:, at], gcol.at[s], gsem.at[s]).start()

    fetch(0, 0)

    @pl.loop(0, NJ)
    def _(i):
        s = lax.rem(i, 2)

        @pl.when(i >= 2)
        def _():
            landed(ogu.at[s], gusem.at[s])
            landed(od.at[s], dsem.at[s])

        @pl.when(i + 1 < NJ)
        def _():
            fetch(i + 1, 1 - s)

        landed(xcol.at[s], xsem.at[s])
        landed(gcol.at[s], gsem.at[s])
        at = pl.ds(pl.multiple_of(i * 256, 256), 256)
        xc = xcol[s]
        ogu[s, 0] = dot(xc, gg[...].reshape(ROWS, FF), 0, 0).astype(BF)
        ogu[s, 1] = dot(xc, ug[...].reshape(ROWS, FF), 0, 0).astype(BF)
        od[s] = dot(hid[...].reshape(ROWS, FF), gcol[s], 0, 0).astype(BF)
        pltpu.make_async_copy(ogu.at[s, 0], dg_o.at[at, :], gusem.at[s]).start()
        pltpu.make_async_copy(ogu.at[s, 1], du_o.at[at, :], gusem.at[s]).start()
        pltpu.make_async_copy(od.at[s], dd_o.at[:, at], dsem.at[s]).start()

        j = lax.rem(own + 4 + i, NJ)
        landed(rrp.at[j], p1r.at[j])
        hots = slots_of(rank_ref, j)
        for c in range(0, DP, 512):
            part[j, :, c : c + 512] = dot(hots, rrp[j, :, c : c + 512], 0, 0).astype(BF)

        @pl.when(i != 4)
        def _():
            send(part.at[j], rrz.at[own], p2s.at[j], p2r.at[own], (grp, j))

        @pl.when(i == 4)
        def _():
            pltpu.make_async_copy(part.at[j], rrz.at[j], p2r.at[j]).start()

        for h in range(2):
            d = 2 * i + h
            a = group_to(grp, d)
            landed(rrq.at[a], t1r.at[a])
            hot = jnp.where(spot == pos_ref[a, 0:1, :], 1.0, 0.0).astype(BF)
            for c in range(0, D - DP, 512):
                s2[a, :, c : c + 512] = dot(hot, rrq[a, :, c : c + 512]).astype(BF)

            if h == 0:
                @pl.when(d > 0)
                def _():
                    send(s2.at[a], rr2.at[grp], t2s.at[a], t2r.at[grp], (a, own))

                @pl.when(d == 0)
                def _():
                    pltpu.make_async_copy(s2.at[a], rr2.at[a], t2r.at[a]).start()
            else:
                send(s2.at[a], rr2.at[grp], t2s.at[a], t2r.at[grp], (a, own))

    for j in range(NJ):
        landed(rrz.at[j], p2r.at[j])
    for c in range(0, DP, 512):
        total = rrz[0, :, c : c + 512].astype(F32)
        for j in range(1, NJ):
            total = total + rrz[j, :, c : c + 512].astype(F32)
        gin_o[:, c : c + 512] = total.astype(BF)
    for a in range(NG):
        landed(rr2.at[a], t2r.at[a])
    for c in range(0, D - DP, 512):
        rows = rr2[:, :, c : c + 512].reshape(NG * PG, 512)
        gin_o[:, DP + c : DP + c + 512] = dot(c_ref[...], rows, 0, 0).astype(BF)

    for s in range(2):
        landed(ogu.at[s], gusem.at[s])
        landed(od.at[s], dsem.at[s])
    for a in range(NG):
        landed(dxq.at[a, pl.ds(0, (NJ - 1) * CAP)], t1s.at[a])
    for j in range(NJ):
        landed(dxp.at[j, pl.ds(0, (NG - 1) * CAP)], p1s.at[j])
    for k in range(1, NJ):
        j = lax.rem(own + k, NJ)
        landed(part.at[j], p2s.at[j])
    for d in range(1, NG):
        a = group_to(grp, d)
        landed(s2.at[a], t2s.at[a])


def body(tokens_in, out_grad, expert_ids, gate_weights, w_gate, w_up, w_down):
    hbm = pl.BlockSpec(memory_space=pl.ANY)
    vm = pl.BlockSpec(memory_space=pltpu.VMEM)
    sem = pltpu.SemaphoreType.DMA
    shape = jax.ShapeDtypeStruct
    wg, wu, wd = w_gate[0], w_up[0], w_down[0]
    xr, gr, hid, gg, ug, hots, pos, rank = pl.pallas_call(
        dispatch_kernel,
        name="dispatch",
        out_shape=(
            shape((NJ, NG, CAP, D), BF), shape((NJ, NG, CAP, D), BF),
            shape((NJ, 2 * T, FF), BF), shape((NJ, 2 * T, FF), BF), shape((NJ, 2 * T, FF), BF),
            shape((NG * PG, T), BF), shape((NG, 8, 128), I32), shape((NJ, NG, T), I32),
        ),
        in_specs=[vm, vm, hbm, vm, hbm, hbm, hbm],
        out_specs=(hbm, hbm, hbm, hbm, hbm, vm, vm, vm),
        scratch_shapes=[
            pltpu.VMEM((NJ, T, D), BF),
            pltpu.VMEM((NJ, NG, CAP, D), BF),
            pltpu.VMEM((NG, PG, D), BF),
            pltpu.VMEM((NG, PG, D), BF),
            pltpu.VMEM((NG, NJ * CAP, D), BF),
            pltpu.VMEM((2, NG, CAP, D), BF),
            pltpu.VMEM((2, NG, CAP, D), BF),
            pltpu.VMEM((D, FF), BF), pltpu.VMEM((D, FF), BF), pltpu.VMEM((FF, D), BF),
            pltpu.VMEM((2, 3, 2 * T, FF), BF),
            pltpu.VMEM((NJ, NG, T), I32), pltpu.VMEM((NJ, NG, T), I32),
            pltpu.VMEM((NG, 8, 128), I32), pltpu.VMEM((NG, 8, 128), I32),
            pltpu.VMEM((E, T), I32), pltpu.VMEM((E, T), F32),
            sem((7,)), sem((NJ,)), sem((NJ,)), sem((NJ,)),
            sem((NG,)), sem((NG,)), sem((NG,)), sem((NG,)), sem((NG,)), sem((NG,)),
            sem((NG,)), sem((NG,)), sem((3,)), sem((2,)), sem((2,)), sem((2,)),
        ],
        compiler_params=pltpu.CompilerParams(
            collective_id=0, has_side_effects=True, vmem_limit_bytes=VMEM_LIMIT
        ),
    )(expert_ids.T, gate_weights.T, tokens_in, out_grad, wg, wu, wd)
    grad_in, d_gate, d_up, d_down = pl.pallas_call(
        combine_kernel,
        name="combine",
        out_shape=(
            shape((T, D), BF), shape((D, FF), BF), shape((D, FF), BF), shape((FF, D), BF),
        ),
        in_specs=[vm, vm, vm] + [hbm] * 7,
        out_specs=(vm, hbm, hbm, hbm),
        scratch_shapes=[
            pltpu.VMEM((NJ, 2 * T, FF), BF), pltpu.VMEM((NJ, 2 * T, FF), BF),
            pltpu.VMEM((NJ, 2 * T, FF), BF),
            pltpu.VMEM((D, FF), BF), pltpu.VMEM((D, FF), BF),
            pltpu.VMEM((NJ, 2 * T, DP), BF),
            pltpu.VMEM((NG, T, D - DP), BF),
            pltpu.VMEM((NJ, 2 * T, DP), BF),
            pltpu.VMEM((NG, T, D - DP), BF),
            pltpu.VMEM((NJ, T, DP), BF),
            pltpu.VMEM((NJ, T, DP), BF),
            pltpu.VMEM((NG, PG, D - DP), BF),
            pltpu.VMEM((NG, PG, D - DP), BF),
            pltpu.VMEM((2, ROWS, 256), BF), pltpu.VMEM((2, ROWS, 256), BF),
            pltpu.VMEM((2, 2, 256, FF), BF), pltpu.VMEM((2, FF, 256), BF),
            sem((5,)), sem((NJ,)), sem((NJ,)), sem((NJ,)), sem((NJ,)),
            sem((NG,)), sem((NG,)), sem((NG,)), sem((NG,)),
            sem((2,)), sem((2,)), sem((2,)), sem((2,)),
        ],
        compiler_params=pltpu.CompilerParams(
            collective_id=1, has_side_effects=True, vmem_limit_bytes=VMEM_LIMIT
        ),
    )(hots, pos, rank, xr.reshape(ROWS, D), gr.reshape(ROWS, D), hid, gg, ug, wg, wu)
    return grad_in, d_gate[None], d_up[None], d_down[None]


def solution(mesh):
    both = ("group", "expert")
    return jax.shard_map(
        body,
        mesh=mesh,
        in_specs=(P(both, None),) * 4 + (P(both, None, None),) * 3,
        out_specs=(P(both, None),) + (P(both, None, None),) * 3,
        check_vma=False,
    )
```

```python
import jax
import jax.numpy as jnp
from jax import lax
from jax.experimental import pallas as pl
from jax.experimental.pallas import tpu as pltpu
from jax.sharding import PartitionSpec as P

NG, NJ = 16, 8
T, D, FF = 128, 2048, 768
CAP = 16
PG = 64
E = NG * NJ
DP = 1024
ROWS = NG * NJ * CAP
BF, F32, I32 = jnp.bfloat16, jnp.float32, jnp.int32
MESH = pl.DeviceIdType.MESH
VMEM_LIMIT = 67043328


def dot(a, b, ca=1, cb=0):
    return lax.dot_general(a, b, (((ca,), (cb,)), ((), ())), preferred_element_type=F32)


NEAR = ((0, 1), (1, 0), (0, 3), (3, 0))
DIAG = ((1, 1), (3, 3), (1, 3), (3, 1))
LONG = ((1, 2), (2, 1), (3, 2), (2, 3))
FAR = ((2, 2), (0, 2), (2, 0))
SETS = (NEAR, DIAG, LONG, FAR + ((0, 0),))
OUTWARD = FAR[:1] + LONG + FAR[1:] + DIAG + NEAR


def shift_of(d):
    if isinstance(d, tuple):
        return d
    if isinstance(d, int):
        return d % 4, (d // 4 + d % 4) % 4
    dy = lax.rem(d, 4)
    return dy, lax.rem(lax.div(d, 4) + dy, 4)


def group_to(grp, d):
    dy, dx = shift_of(d)
    return lax.rem(lax.div(grp, 4) + dy, 4) * 4 + lax.rem(lax.rem(grp, 4) + dx, 4)


def group_from(grp, d):
    dy, dx = shift_of(d)
    return lax.rem(lax.div(grp, 4) - dy + 4, 4) * 4 + lax.rem(lax.rem(grp, 4) - dx + 4, 4)


def enter(grp, own):
    barrier = pltpu.get_barrier_semaphore()
    for d in range(1, NG):
        pl.semaphore_signal(barrier, inc=1, device_id=(group_to(grp, d), own), device_id_type=MESH)
    for k in range(1, NJ):
        pl.semaphore_signal(
            barrier, inc=1, device_id=(grp, lax.rem(own + k, NJ)), device_id_type=MESH
        )
    return barrier


def send(src, dst, ssem, rsem, device):
    pltpu.make_async_remote_copy(
        src_ref=src, dst_ref=dst, send_sem=ssem, recv_sem=rsem,
        device_id=device, device_id_type=MESH,
    ).start()


def landed(ref, sem):
    pltpu.make_async_copy(ref, ref, sem).wait()


def iota(shape, dim):
    return lax.broadcasted_iota(I32, shape, dim)


def slots_of(rank_ref, j):
    spot = iota((CAP, T), 0)
    return jnp.concatenate(
        [jnp.where(spot == rank_ref[j, a : a + 1, :], 1.0, 0.0).astype(BF) for a in range(NG)],
        axis=0,
    )


def dispatch_kernel(
    ids_ref, gw_ref, x_hbm, g_ref, wg_hbm, wu_hbm, wd_hbm,
    xr, gr, hid_o, gg_o, ug_o, c_o, pos_o, rank_o,
    ax, pbuf, s1, r1, s2, stx, stg, wg, wu, wd, ost,
    rank_s, rank_r, pos_s, pos_r, post, wt,
    axs, axr, ms, mr, ps, pr, q1s, q1r, q2s, q2r, p2s, p2r, wsem, xsem, gsem, osem,
):
    grp, own = lax.axis_index("group"), lax.axis_index("expert")
    partner = own + 1 - 2 * lax.rem(own, 2)
    barrier = enter(grp, own)
    loads = [
        pltpu.make_async_copy(wg_hbm, wg, wsem.at[0]),
        pltpu.make_async_copy(wu_hbm, wu, wsem.at[1]),
        pltpu.make_async_copy(wd_hbm, wd, wsem.at[2]),
    ]
    pltpu.make_async_copy(x_hbm, ax.at[own], axr.at[own]).start()

    row, lane = iota((E, T), 0), iota((E, T), 1)
    before = jnp.where(row < lane, 1.0, 0.0).astype(BF)
    named = jnp.zeros((E, T), F32)
    weight = jnp.zeros((E, T), F32)
    named_p = jnp.zeros((E, T), F32)
    row_p = lax.rem(row, NG) * NJ + lax.div(row, NG)
    for k in range(8):
        idk = ids_ref[k : k + 1, :]
        gwk = gw_ref[k : k + 1, :]
        named = jnp.where(row == idk, 1.0, named)
        weight = jnp.where(row == idk, gwk, weight)
        named_p = jnp.where(row_p == idk, 1.0, named_p)
    rank = dot(named.astype(BF), before)
    rank_p = dot(named_p.astype(BF), before)
    counts = dot(named.astype(BF), jnp.ones((T, T), BF))
    ahead = jnp.where(
        (lax.div(row, NJ) == lax.div(lane, NJ)) & (lane < row), 1.0, 0.0
    ).astype(BF)
    starts = dot(ahead, counts.astype(BF))
    post[...] = jnp.where(named > 0.5, starts + rank, -1.0).astype(I32)
    wt[...] = weight
    rank_s[...] = jnp.where(named_p > 0.5, rank_p, -1.0).astype(I32).reshape(NJ, NG, T)
    mine = lax.rem(row, NJ) == lax.div(lane, CAP)
    pick = jnp.where(lax.div(iota((NG, E), 1), NJ) == iota((NG, E), 0), 1.0, 0.0).astype(BF)
    start_row = dot(pick, jnp.where(mine, starts, 0.0).astype(BF))
    count_row = dot(pick, jnp.where(mine, counts, 0.0).astype(BF))
    slot = lax.rem(iota((NG, E), 1), CAP).astype(F32)
    pos = jnp.where(slot < count_row, start_row + slot, -1.0).astype(I32)
    for a in range(NG):
        pos_s[a] = jnp.broadcast_to(pos[a : a + 1, :], (8, 128))
    rank_r[own] = rank_s[own]
    pos_r[grp] = pos_s[grp]

    pl.semaphore_wait(barrier, NG + NJ - 2)

    for k in range(1, NJ):
        to = lax.rem(own + k, NJ)
        send(rank_s.at[to], rank_r.at[own], ms.at[k], mr.at[own], (grp, to))
    for i in range(1, 4):
        to = lax.rem(own + 2 * i, NJ)
        send(x_hbm, ax.at[own], axs.at[i], axr.at[own], (grp, to))
    send(x_hbm, ax.at[own], axs.at[0], axr.at[own], (grp, partner))

    spot = iota((PG, T), 0)
    for steps in SETS:
        picks, scales = [], []
        for d in steps:
            a = group_to(grp, d)
            at = pl.ds(pl.multiple_of(a * NJ, NJ), NJ)
            prow, wrow = post[at, :], wt[at, :]
            hot = jnp.zeros((PG, T), F32)
            wsel = jnp.zeros((PG, T), F32)
            for e in range(NJ):
                hit = spot == prow[e : e + 1, :]
                hot = jnp.where(hit, 1.0, hot)
                wsel = jnp.where(hit, wrow[e : e + 1, :], wsel)
            c_o[pl.ds(pl.multiple_of(a * PG, PG), PG), :] = hot.astype(BF)
            picks.append(hot.astype(BF))
            scales.append(jnp.sum(wsel, axis=1, keepdims=True))
        hots = jnp.concatenate(picks, axis=0)
        scale = jnp.concatenate(scales, axis=0)
        for c in range(0, D, 512):
            part = (scale * dot(hots, g_ref[:, c : c + 512])).astype(BF)
            for q, d in enumerate(steps):
                s1[group_to(grp, d), :, c : c + 512] = part[q * PG : (q + 1) * PG, :]
        ends = [d for d in steps if d != (0, 0)]
        for d in ends:
            a = group_to(grp, d)
            send(pos_s.at[a], pos_r.at[grp], ps.at[a], pr.at[grp], (a, own))
        for r in range(0, PG, 16):
            for d in ends:
                a = group_to(grp, d)
                send(s1.at[a, pl.ds(r, 16)], r1.at[grp, pl.ds(r, 16)],
                     q1s.at[a], q1r.at[grp], (a, own))
    for w in loads:
        w.start()

    def spread(a, rows_ref):
        hot = jnp.where(spot == pos_r[a, 0:1, :], 1.0, 0.0).astype(BF)
        for c in range(0, D, 512):
            s2[a, :, c : c + 512] = dot(hot, rows_ref[a, :, c : c + 512], 0, 0).astype(BF)
        for k in range(1, NJ):
            to = lax.rem(own + k, NJ)
            at = pl.ds(pl.multiple_of(to * CAP, CAP), CAP)
            send(s2.at[a, at], gr.at[own, a], q2s.at[a], q2r.at[own], (grp, to))
        at = pl.ds(pl.multiple_of(own * CAP, CAP), CAP)
        pltpu.make_async_copy(s2.at[a, at], gr.at[own, a], q2r.at[own]).start()

    spread(grp, s1)

    for k in range(1, NJ):
        frm = lax.rem(own + k, NJ)
        landed(rank_r.at[frm], mr.at[frm])

    def source(n):
        side = lax.rem(n, 2)
        return lax.rem(own + (partner - own) * side - (n - side) + NJ, NJ)

    @pl.loop(0, NJ)
    def _(n):
        j = source(n)
        landed(ax.at[j], axr.at[j])

        @pl.when((n >= 2) & (lax.rem(n, 2) == 0))
        def _():
            send(ax.at[j], ax.at[j], axs.at[3 + lax.div(n, 2)], axr.at[j], (grp, partner))

        hots = slots_of(rank_r, j)
        for c in range(0, D, 512):
            part = dot(hots, ax[j, :, c : c + 512]).astype(BF)
            pbuf[j, :, :, c : c + 512] = part.reshape(NG, CAP, 512)
        for d in OUTWARD:
            a = group_to(grp, d)
            send(pbuf.at[j, a], xr.at[j, grp], p2s.at[j], p2r.at[j], (a, own))
        pltpu.make_async_copy(pbuf.at[j, grp], xr.at[j, grp], p2r.at[j]).start()

    for steps in SETS:
        for d in steps:
            if d != (0, 0):
                a = group_from(grp, d)
                landed(pos_r.at[a], pr.at[a])
                landed(r1.at[a], q1r.at[a])
                spread(a, r1)

    for w in loads:
        w.wait()

    @pl.loop(0, NJ)
    def _(n):
        j = source(n)
        landed(xr.at[j], p2r.at[j])
        landed(gr.at[j], q2r.at[j])
        x_in = pltpu.make_async_copy(xr.at[j], stx, xsem.at[0])
        g_in = pltpu.make_async_copy(gr.at[j], stg, gsem.at[0])
        x_in.start()
        g_in.start()
        x_in.wait()
        g_in.wait()
        xb = stx[...].reshape(2 * T, D)
        gate_pre = dot(xb, wg[...])
        up_pre = dot(xb, wu[...])
        hgrad = dot(stg[...].reshape(2 * T, D), wd[...], 1, 1)
        sigma = jax.nn.sigmoid(gate_pre)
        act = gate_pre * sigma
        slot_n = lax.rem(n, 2)

        @pl.when(n >= 2)
        def _():
            landed(ost.at[slot_n], osem.at[slot_n])

        ost[slot_n] = (act * up_pre).astype(BF)
        pltpu.make_async_copy(ost.at[slot_n], hid_o.at[j], osem.at[slot_n]).start()
        gg_o[j] = (hgrad * up_pre * sigma * (1.0 + gate_pre * (1.0 - sigma))).astype(BF)
        ug_o[j] = (hgrad * act).astype(BF)

    for n in range(2):
        landed(ost.at[n], osem.at[n])
    pos_o[...] = pos_r[...]
    rank_o[...] = rank_r[...]
    for k in range(1, NJ):
        to = lax.rem(own + k, NJ)
        landed(rank_s.at[to], ms.at[k])
    for i in range(7):
        landed(x_hbm, axs.at[i])
    for d in range(1, NG):
        a = group_to(grp, d)
        landed(pos_s.at[a], ps.at[a])
        landed(s1.at[a], q1s.at[a])
    for j in range(NJ):
        landed(pbuf.at[j, pl.ds(0, NG - 1)], p2s.at[j])
    for a in range(NG):
        landed(s2.at[a, pl.ds(0, (NJ - 1) * CAP)], q2s.at[a])


def combine_kernel(
    c_ref, pos_ref, rank_ref, xr, gr, hid_hbm, gg, ug, wg_hbm, wu_hbm,
    gin_o, dg_o, du_o, dd_o,
    hid, wg, wu, dxp, dxq, rrp, rrq, part, rrz, s2, rr2, xcol, gcol,
    wsem, p1s, p1r, p2s, p2r, t1s, t1r, t2s, t2r, xsem, gsem,
):
    grp, own = lax.axis_index("group"), lax.axis_index("expert")
    barrier = enter(grp, own)
    loads = [
        pltpu.make_async_copy(wg_hbm, wg, wsem.at[0]),
        pltpu.make_async_copy(wu_hbm, wu, wsem.at[1]),
        pltpu.make_async_copy(hid_hbm, hid, wsem.at[2]),
    ]
    for w in loads:
        w.start()
    for w in loads[:2]:
        w.wait()

    def slot_rows(a):
        return pl.ds(pl.multiple_of(a * CAP, CAP), CAP)

    def input_rows(ggb, ugb, c):
        return (
            dot(ggb, wg[c : c + 512, :], 1, 1) + dot(ugb, wu[c : c + 512, :], 1, 1)
        ).astype(BF)

    def make_rows(n):
        j = lax.rem(own + 4 + n, NJ)
        for c in range(0, DP, 512):
            dxp[j, :, c : c + 512] = input_rows(gg[j], ug[j], c)
        tops = [group_to(grp, 2 * n + h) for h in range(2)]
        ats = [slot_rows(a) for a in tops]
        ggb = jnp.concatenate([gg[q, at, :] for at in ats for q in range(NJ)], axis=0)
        ugb = jnp.concatenate([ug[q, at, :] for at in ats for q in range(NJ)], axis=0)
        for c in range(DP, D, 512):
            rows = input_rows(ggb, ugb, c)
            for h in range(2):
                dxq[tops[h], :, c - DP : c - DP + 512] = rows[h * T : (h + 1) * T, :]

    def send_rows(n):
        j = lax.rem(own + 4 + n, NJ)
        for d in OUTWARD:
            a = group_to(grp, d)
            send(dxp.at[j, slot_rows(a)], rrp.at[j, slot_rows(grp)],
                 p1s.at[j], p1r.at[j], (a, own))
        pltpu.make_async_copy(
            dxp.at[j, slot_rows(grp)], rrp.at[j, slot_rows(grp)], p1r.at[j]
        ).start()
        for h in range(2):
            a = group_to(grp, 2 * n + h)
            for k in range(1, NJ):
                to = lax.rem(own + k, NJ)
                send(dxq.at[a, slot_rows(to)], rrq.at[a, slot_rows(own)],
                     t1s.at[a], t1r.at[a], (grp, to))
            pltpu.make_async_copy(
                dxq.at[a, slot_rows(own)], rrq.at[a, slot_rows(own)], t1r.at[a]
            ).start()

    make_rows(0)
    pl.semaphore_wait(barrier, NG + NJ - 2)
    send_rows(0)

    @pl.loop(1, NJ)
    def _(n):
        make_rows(n)
        send_rows(n)

    loads[2].wait()
    spot = iota((PG, T), 0)

    def fetch(c, s):
        at = pl.ds(pl.multiple_of(c * 256, 256), 256)
        pltpu.make_async_copy(xr.at[:, at], xcol.at[s], xsem.at[s]).start()
        pltpu.make_async_copy(gr.at[:, at], gcol.at[s], gsem.at[s]).start()

    fetch(0, 0)

    @pl.loop(0, NJ)
    def _(i):
        s = lax.rem(i, 2)

        @pl.when(i + 1 < NJ)
        def _():
            fetch(i + 1, 1 - s)

        landed(xcol.at[s], xsem.at[s])
        landed(gcol.at[s], gsem.at[s])
        at = pl.ds(pl.multiple_of(i * 256, 256), 256)
        xc = xcol[s]
        dg_o[at, :] = dot(xc, gg[...].reshape(ROWS, FF), 0, 0).astype(BF)
        du_o[at, :] = dot(xc, ug[...].reshape(ROWS, FF), 0, 0).astype(BF)
        dd_o[:, at] = dot(hid[...].reshape(ROWS, FF), gcol[s], 0, 0).astype(BF)

        j = lax.rem(own + 4 + i, NJ)
        landed(rrp.at[j], p1r.at[j])
        hots = slots_of(rank_ref, j)
        for c in range(0, DP, 512):
            part[j, :, c : c + 512] = dot(hots, rrp[j, :, c : c + 512], 0, 0).astype(BF)

        @pl.when(i != 4)
        def _():
            send(part.at[j], rrz.at[own], p2s.at[j], p2r.at[own], (grp, j))

        @pl.when(i == 4)
        def _():
            pltpu.make_async_copy(part.at[j], rrz.at[j], p2r.at[j]).start()

        for h in range(2):
            d = 2 * i + h
            a = group_to(grp, d)
            landed(rrq.at[a], t1r.at[a])
            hot = jnp.where(spot == pos_ref[a, 0:1, :], 1.0, 0.0).astype(BF)
            for c in range(0, D - DP, 512):
                s2[a, :, c : c + 512] = dot(hot, rrq[a, :, c : c + 512]).astype(BF)

            if h == 0:
                @pl.when(d > 0)
                def _():
                    send(s2.at[a], rr2.at[grp], t2s.at[a], t2r.at[grp], (a, own))

                @pl.when(d == 0)
                def _():
                    pltpu.make_async_copy(s2.at[a], rr2.at[a], t2r.at[a]).start()
            else:
                send(s2.at[a], rr2.at[grp], t2s.at[a], t2r.at[grp], (a, own))

    for j in range(NJ):
        landed(rrz.at[j], p2r.at[j])
    for c in range(0, DP, 512):
        total = rrz[0, :, c : c + 512].astype(F32)
        for j in range(1, NJ):
            total = total + rrz[j, :, c : c + 512].astype(F32)
        gin_o[:, c : c + 512] = total.astype(BF)
    for a in range(NG):
        landed(rr2.at[a], t2r.at[a])
    for c in range(0, D - DP, 512):
        rows = rr2[:, :, c : c + 512].reshape(NG * PG, 512)
        gin_o[:, DP + c : DP + c + 512] = dot(c_ref[...], rows, 0, 0).astype(BF)

    for a in range(NG):
        landed(dxq.at[a, pl.ds(0, (NJ - 1) * CAP)], t1s.at[a])
    for j in range(NJ):
        landed(dxp.at[j, pl.ds(0, (NG - 1) * CAP)], p1s.at[j])
    for k in range(1, NJ):
        j = lax.rem(own + k, NJ)
        landed(part.at[j], p2s.at[j])
    for d in range(1, NG):
        a = group_to(grp, d)
        landed(s2.at[a], t2s.at[a])


def body(tokens_in, out_grad, expert_ids, gate_weights, w_gate, w_up, w_down):
    hbm = pl.BlockSpec(memory_space=pl.ANY)
    vm = pl.BlockSpec(memory_space=pltpu.VMEM)
    sem = pltpu.SemaphoreType.DMA
    shape = jax.ShapeDtypeStruct
    wg, wu, wd = w_gate[0], w_up[0], w_down[0]
    xr, gr, hid, gg, ug, hots, pos, rank = pl.pallas_call(
        dispatch_kernel,
        name="dispatch",
        out_shape=(
            shape((NJ, NG, CAP, D), BF), shape((NJ, NG, CAP, D), BF),
            shape((NJ, 2 * T, FF), BF), pltpu.VMEM((NJ, 2 * T, FF), BF),
            pltpu.VMEM((NJ, 2 * T, FF), BF),
            pltpu.VMEM((NG * PG, T), BF), pltpu.VMEM((NG, 8, 128), I32),
            pltpu.VMEM((NJ, NG, T), I32),
        ),
        in_specs=[vm, vm, hbm, vm, hbm, hbm, hbm],
        out_specs=(hbm, hbm, hbm) + (vm,) * 5,
        scratch_shapes=[
            pltpu.VMEM((NJ, T, D), BF),
            pltpu.VMEM((NJ, NG, CAP, D), BF),
            pltpu.VMEM((NG, PG, D), BF),
            pltpu.VMEM((NG, PG, D), BF),
            pltpu.VMEM((NG, NJ * CAP, D), BF),
            pltpu.VMEM((NG, CAP, D), BF),
            pltpu.VMEM((NG, CAP, D), BF),
            pltpu.VMEM((D, FF), BF), pltpu.VMEM((D, FF), BF), pltpu.VMEM((FF, D), BF),
            pltpu.VMEM((2, 2 * T, FF), BF),
            pltpu.VMEM((NJ, NG, T), I32), pltpu.VMEM((NJ, NG, T), I32),
            pltpu.VMEM((NG, 8, 128), I32), pltpu.VMEM((NG, 8, 128), I32),
            pltpu.VMEM((E, T), I32), pltpu.VMEM((E, T), F32),
            sem((7,)), sem((NJ,)), sem((NJ,)), sem((NJ,)),
            sem((NG,)), sem((NG,)), sem((NG,)), sem((NG,)), sem((NG,)), sem((NG,)),
            sem((NG,)), sem((NG,)), sem((3,)), sem((1,)), sem((1,)), sem((2,)),
        ],
        compiler_params=pltpu.CompilerParams(
            collective_id=0, has_side_effects=True, vmem_limit_bytes=48 << 20
        ),
    )(expert_ids.T, gate_weights.T, tokens_in, out_grad, wg, wu, wd)
    grad_in, d_gate, d_up, d_down = pl.pallas_call(
        combine_kernel,
        name="combine",
        out_shape=(
            pltpu.VMEM((T, D), BF), pltpu.VMEM((D, FF), BF),
            pltpu.VMEM((D, FF), BF), pltpu.VMEM((FF, D), BF),
        ),
        in_specs=[vm, vm, vm, hbm, hbm, hbm, vm, vm, hbm, hbm],
        out_specs=(vm, vm, vm, vm),
        scratch_shapes=[
            pltpu.VMEM((NJ, 2 * T, FF), BF),
            pltpu.VMEM((D, FF), BF), pltpu.VMEM((D, FF), BF),
            pltpu.VMEM((NJ, 2 * T, DP), BF),
            pltpu.VMEM((NG, T, D - DP), BF),
            pltpu.VMEM((NJ, 2 * T, DP), BF),
            pltpu.VMEM((NG, T, D - DP), BF),
            pltpu.VMEM((NJ, T, DP), BF),
            pltpu.VMEM((NJ, T, DP), BF),
            pltpu.VMEM((NG, PG, D - DP), BF),
            pltpu.VMEM((NG, PG, D - DP), BF),
            pltpu.VMEM((2, ROWS, 256), BF), pltpu.VMEM((2, ROWS, 256), BF),
            sem((3,)), sem((NJ,)), sem((NJ,)), sem((NJ,)), sem((NJ,)),
            sem((NG,)), sem((NG,)), sem((NG,)), sem((NG,)),
            sem((2,)), sem((2,)),
        ],
        compiler_params=pltpu.CompilerParams(
            collective_id=1, has_side_effects=True, vmem_limit_bytes=42 << 20
        ),
    )(*[pltpu.with_memory_space_constraint(v, pltpu.VMEM) for v in (hots, pos, rank)], xr.reshape(ROWS, D), gr.reshape(ROWS, D), hid,
      *[pltpu.with_memory_space_constraint(v, pltpu.VMEM) for v in (gg, ug)],
      wg, wu)
    return grad_in, d_gate[None], d_up[None], d_down[None]


def solution(mesh):
    both = ("group", "expert")
    return jax.shard_map(
        body,
        mesh=mesh,
        in_specs=(P(both, None),) * 4 + (P(both, None, None),) * 3,
        out_specs=(P(both, None),) + (P(both, None, None),) * 3,
        check_vma=False,
    )
```

```python
import jax
import jax.numpy as jnp
from jax import lax
from jax.experimental import pallas as pl
from jax.experimental.pallas import tpu as pltpu
from jax.sharding import PartitionSpec as P

NG, NJ = 16, 8
T, D, FF = 128, 2048, 768
CAP = 16
PG = 64
E = NG * NJ
DP = 1024
ROWS = NG * NJ * CAP
BF, F32, I32 = jnp.bfloat16, jnp.float32, jnp.int32
MESH = pl.DeviceIdType.MESH
VMEM_LIMIT = 67043328


def dot(a, b, ca=1, cb=0):
    return lax.dot_general(a, b, (((ca,), (cb,)), ((), ())), preferred_element_type=F32)


NEAR = ((0, 1), (1, 0), (0, 3), (3, 0))
DIAG = ((1, 1), (3, 3), (1, 3), (3, 1))
LONG = ((1, 2), (2, 1), (3, 2), (2, 3))
FAR = ((2, 2), (0, 2), (2, 0))
SETS = (NEAR, DIAG, LONG, FAR + ((0, 0),))
OUTWARD = FAR[:1] + LONG + FAR[1:] + DIAG + NEAR


def shift_of(d):
    if isinstance(d, tuple):
        return d
    if isinstance(d, int):
        return d % 4, (d // 4 + d % 4) % 4
    dy = lax.rem(d, 4)
    return dy, lax.rem(lax.div(d, 4) + dy, 4)


def group_to(grp, d):
    dy, dx = shift_of(d)
    return lax.rem(lax.div(grp, 4) + dy, 4) * 4 + lax.rem(lax.rem(grp, 4) + dx, 4)


def group_from(grp, d):
    dy, dx = shift_of(d)
    return lax.rem(lax.div(grp, 4) - dy + 4, 4) * 4 + lax.rem(lax.rem(grp, 4) - dx + 4, 4)


def enter(grp, own):
    barrier = pltpu.get_barrier_semaphore()
    for d in range(1, NG):
        pl.semaphore_signal(barrier, inc=1, device_id=(group_to(grp, d), own), device_id_type=MESH)
    for k in range(1, NJ):
        pl.semaphore_signal(
            barrier, inc=1, device_id=(grp, lax.rem(own + k, NJ)), device_id_type=MESH
        )
    return barrier


def send(src, dst, ssem, rsem, device):
    pltpu.make_async_remote_copy(
        src_ref=src, dst_ref=dst, send_sem=ssem, recv_sem=rsem,
        device_id=device, device_id_type=MESH,
    ).start()


def landed(ref, sem):
    pltpu.make_async_copy(ref, ref, sem).wait()


def iota(shape, dim):
    return lax.broadcasted_iota(I32, shape, dim)


def slots_of(rank_ref, j):
    spot = iota((CAP, T), 0)
    return jnp.concatenate(
        [jnp.where(spot == rank_ref[j, a : a + 1, :], 1.0, 0.0).astype(BF) for a in range(NG)],
        axis=0,
    )


def dispatch_kernel(
    ids_ref, gw_ref, x_hbm, g_ref, wg_hbm, wu_hbm, wd_hbm,
    xr, gr, hid_o, gg_o, ug_o, c_o, pos_o, rank_o,
    ax, pbuf, s1, r1, s2, stx, stg, wg, wu, wd, ost,
    rank_s, rank_r, pos_s, pos_r, post, wt,
    axs, axr, ms, mr, ps, pr, q1s, q1r, q2s, q2r, p2s, p2r, wsem, xsem, gsem, osem,
):
    grp, own = lax.axis_index("group"), lax.axis_index("expert")
    partner = own + 1 - 2 * lax.rem(own, 2)
    barrier = enter(grp, own)
    loads = [
        pltpu.make_async_copy(wg_hbm, wg, wsem.at[0]),
        pltpu.make_async_copy(wu_hbm, wu, wsem.at[1]),
        pltpu.make_async_copy(wd_hbm, wd, wsem.at[2]),
    ]
    pltpu.make_async_copy(x_hbm, ax.at[own], axr.at[own]).start()

    row, lane = iota((E, T), 0), iota((E, T), 1)
    before = jnp.where(row < lane, 1.0, 0.0).astype(BF)
    named = jnp.zeros((E, T), F32)
    weight = jnp.zeros((E, T), F32)
    named_p = jnp.zeros((E, T), F32)
    row_p = lax.rem(row, NG) * NJ + lax.div(row, NG)
    for k in range(8):
        idk = ids_ref[k : k + 1, :]
        gwk = gw_ref[k : k + 1, :]
        named = jnp.where(row == idk, 1.0, named)
        weight = jnp.where(row == idk, gwk, weight)
        named_p = jnp.where(row_p == idk, 1.0, named_p)
    rank = dot(named.astype(BF), before)
    rank_p = dot(named_p.astype(BF), before)
    counts = dot(named.astype(BF), jnp.ones((T, T), BF))
    ahead = jnp.where(
        (lax.div(row, NJ) == lax.div(lane, NJ)) & (lane < row), 1.0, 0.0
    ).astype(BF)
    starts = dot(ahead, counts.astype(BF))
    post[...] = jnp.where(named > 0.5, starts + rank, -1.0).astype(I32)
    wt[...] = weight
    rank_s[...] = jnp.where(named_p > 0.5, rank_p, -1.0).astype(I32).reshape(NJ, NG, T)
    mine = lax.rem(row, NJ) == lax.div(lane, CAP)
    pick = jnp.where(lax.div(iota((NG, E), 1), NJ) == iota((NG, E), 0), 1.0, 0.0).astype(BF)
    start_row = dot(pick, jnp.where(mine, starts, 0.0).astype(BF))
    count_row = dot(pick, jnp.where(mine, counts, 0.0).astype(BF))
    slot = lax.rem(iota((NG, E), 1), CAP).astype(F32)
    pos = jnp.where(slot < count_row, start_row + slot, -1.0).astype(I32)
    for a in range(NG):
        pos_s[a] = jnp.broadcast_to(pos[a : a + 1, :], (8, 128))
    rank_r[own] = rank_s[own]
    pos_r[grp] = pos_s[grp]

    pl.semaphore_wait(barrier, NG + NJ - 2)

    for k in range(1, NJ):
        to = lax.rem(own + k, NJ)
        send(rank_s.at[to], rank_r.at[own], ms.at[k], mr.at[own], (grp, to))
    for i in range(1, 4):
        to = lax.rem(own + 2 * i, NJ)
        send(x_hbm, ax.at[own], axs.at[i], axr.at[own], (grp, to))
    send(x_hbm, ax.at[own], axs.at[0], axr.at[own], (grp, partner))

    spot = iota((PG, T), 0)
    for steps in SETS:
        picks, scales = [], []
        for d in steps:
            a = group_to(grp, d)
            at = pl.ds(pl.multiple_of(a * NJ, NJ), NJ)
            prow, wrow = post[at, :], wt[at, :]
            hot = jnp.zeros((PG, T), F32)
            wsel = jnp.zeros((PG, T), F32)
            for e in range(NJ):
                hit = spot == prow[e : e + 1, :]
                hot = jnp.where(hit, 1.0, hot)
                wsel = jnp.where(hit, wrow[e : e + 1, :], wsel)
            c_o[pl.ds(pl.multiple_of(a * PG, PG), PG), :] = hot.astype(BF)
            picks.append(hot.astype(BF))
            scales.append(jnp.sum(wsel, axis=1, keepdims=True))
        hots = jnp.concatenate(picks, axis=0)
        scale = jnp.concatenate(scales, axis=0)
        for c in range(0, D, 512):
            part = (scale * dot(hots, g_ref[:, c : c + 512])).astype(BF)
            for q, d in enumerate(steps):
                s1[group_to(grp, d), :, c : c + 512] = part[q * PG : (q + 1) * PG, :]
        ends = [d for d in steps if d != (0, 0)]
        for d in ends:
            a = group_to(grp, d)
            send(pos_s.at[a], pos_r.at[grp], ps.at[a], pr.at[grp], (a, own))
        for r in range(0, PG, 16):
            for d in ends:
                a = group_to(grp, d)
                send(s1.at[a, pl.ds(r, 16)], r1.at[grp, pl.ds(r, 16)],
                     q1s.at[a], q1r.at[grp], (a, own))
    for w in loads:
        w.start()

    def spread(a, rows_ref):
        hot = jnp.where(spot == pos_r[a, 0:1, :], 1.0, 0.0).astype(BF)
        for c in range(0, D, 512):
            s2[a, :, c : c + 512] = dot(hot, rows_ref[a, :, c : c + 512], 0, 0).astype(BF)
        for k in range(1, NJ):
            to = lax.rem(own + k, NJ)
            at = pl.ds(pl.multiple_of(to * CAP, CAP), CAP)
            send(s2.at[a, at], gr.at[own, a], q2s.at[a], q2r.at[own], (grp, to))
        at = pl.ds(pl.multiple_of(own * CAP, CAP), CAP)
        pltpu.make_async_copy(s2.at[a, at], gr.at[own, a], q2r.at[own]).start()

    spread(grp, s1)

    for k in range(1, NJ):
        frm = lax.rem(own + k, NJ)
        landed(rank_r.at[frm], mr.at[frm])

    def source(n):
        side = lax.rem(n, 2)
        return lax.rem(own + (partner - own) * side - (n - side) + NJ, NJ)

    @pl.loop(0, NJ)
    def _(n):
        j = source(n)
        landed(ax.at[j], axr.at[j])

        @pl.when((n >= 2) & (lax.rem(n, 2) == 0))
        def _():
            send(ax.at[j], ax.at[j], axs.at[3 + lax.div(n, 2)], axr.at[j], (grp, partner))

        hots = slots_of(rank_r, j)
        for c in range(0, D, 512):
            part = dot(hots, ax[j, :, c : c + 512]).astype(BF)
            pbuf[j, :, :, c : c + 512] = part.reshape(NG, CAP, 512)
        for d in OUTWARD:
            a = group_to(grp, d)
            send(pbuf.at[j, a], xr.at[j, grp], p2s.at[j], p2r.at[j], (a, own))
        pltpu.make_async_copy(pbuf.at[j, grp], xr.at[j, grp], p2r.at[j]).start()

    for steps in SETS:
        for d in steps:
            if d != (0, 0):
                a = group_from(grp, d)
                landed(pos_r.at[a], pr.at[a])
                landed(r1.at[a], q1r.at[a])
                spread(a, r1)

    for w in loads:
        w.wait()

    @pl.loop(0, NJ)
    def _(n):
        j = source(n)
        landed(xr.at[j], p2r.at[j])
        landed(gr.at[j], q2r.at[j])
        x_in = pltpu.make_async_copy(xr.at[j], stx, xsem.at[0])
        g_in = pltpu.make_async_copy(gr.at[j], stg, gsem.at[0])
        x_in.start()
        g_in.start()
        x_in.wait()
        g_in.wait()
        xb = stx[...].reshape(2 * T, D)
        gate_pre = dot(xb, wg[...])
        up_pre = dot(xb, wu[...])
        hgrad = dot(stg[...].reshape(2 * T, D), wd[...], 1, 1)
        sigma = jax.nn.sigmoid(gate_pre)
        act = gate_pre * sigma
        slot_n = lax.rem(n, 2)

        @pl.when(n >= 2)
        def _():
            landed(ost.at[slot_n], osem.at[slot_n])

        ost[slot_n] = (act * up_pre).astype(BF)
        pltpu.make_async_copy(ost.at[slot_n], hid_o.at[j], osem.at[slot_n]).start()
        gg_o[j] = (hgrad * up_pre * sigma * (1.0 + gate_pre * (1.0 - sigma))).astype(BF)
        ug_o[j] = (hgrad * act).astype(BF)

    for n in range(2):
        landed(ost.at[n], osem.at[n])
    pos_o[...] = pos_r[...]
    rank_o[...] = rank_r[...]
    for k in range(1, NJ):
        to = lax.rem(own + k, NJ)
        landed(rank_s.at[to], ms.at[k])
    for i in range(7):
        landed(x_hbm, axs.at[i])
    for d in range(1, NG):
        a = group_to(grp, d)
        landed(pos_s.at[a], ps.at[a])
        landed(s1.at[a], q1s.at[a])
    for j in range(NJ):
        landed(pbuf.at[j, pl.ds(0, NG - 1)], p2s.at[j])
    for a in range(NG):
        landed(s2.at[a, pl.ds(0, (NJ - 1) * CAP)], q2s.at[a])


def combine_kernel(
    c_ref, pos_ref, rank_ref, xr, gr, hid_hbm, gg, ug, wg_hbm, wu_hbm,
    gin_o, dg_o, du_o, dd_o,
    hid, wg, wu, dxp, dxq, rrp, rrq, part, rrz, s2, rr2, xcol, gcol,
    wsem, p1s, p1r, p2s, p2r, t1s, t1r, t2s, t2r, xsem, gsem,
):
    grp, own = lax.axis_index("group"), lax.axis_index("expert")
    barrier = enter(grp, own)
    loads = [
        pltpu.make_async_copy(wg_hbm, wg, wsem.at[0]),
        pltpu.make_async_copy(wu_hbm, wu, wsem.at[1]),
        pltpu.make_async_copy(hid_hbm, hid, wsem.at[2]),
    ]
    for w in loads:
        w.start()
    for w in loads[:2]:
        w.wait()

    def slot_rows(a):
        return pl.ds(pl.multiple_of(a * CAP, CAP), CAP)

    def input_rows(ggb, ugb, c):
        return (
            dot(ggb, wg[c : c + 512, :], 1, 1) + dot(ugb, wu[c : c + 512, :], 1, 1)
        ).astype(BF)

    def make_rows(n):
        j = lax.rem(own + 4 + n, NJ)
        for c in range(0, DP, 512):
            dxp[j, :, c : c + 512] = input_rows(gg[j], ug[j], c)
        tops = [group_to(grp, 2 * n + h) for h in range(2)]
        ats = [slot_rows(a) for a in tops]
        ggb = jnp.concatenate([gg[q, at, :] for at in ats for q in range(NJ)], axis=0)
        ugb = jnp.concatenate([ug[q, at, :] for at in ats for q in range(NJ)], axis=0)
        for c in range(DP, D, 512):
            rows = input_rows(ggb, ugb, c)
            for h in range(2):
                dxq[tops[h], :, c - DP : c - DP + 512] = rows[h * T : (h + 1) * T, :]

    def send_rows(n):
        j = lax.rem(own + 4 + n, NJ)
        for d in OUTWARD:
            a = group_to(grp, d)
            send(dxp.at[j, slot_rows(a)], rrp.at[j, slot_rows(grp)],
                 p1s.at[j], p1r.at[j], (a, own))
        pltpu.make_async_copy(
            dxp.at[j, slot_rows(grp)], rrp.at[j, slot_rows(grp)], p1r.at[j]
        ).start()
        for h in range(2):
            a = group_to(grp, 2 * n + h)
            for k in range(1, NJ):
                to = lax.rem(own + k, NJ)
                send(dxq.at[a, slot_rows(to)], rrq.at[a, slot_rows(own)],
                     t1s.at[a], t1r.at[a], (grp, to))
            pltpu.make_async_copy(
                dxq.at[a, slot_rows(own)], rrq.at[a, slot_rows(own)], t1r.at[a]
            ).start()

    make_rows(0)
    pl.semaphore_wait(barrier, NG + NJ - 2)
    send_rows(0)

    @pl.loop(1, NJ)
    def _(n):
        make_rows(n)
        send_rows(n)

    loads[2].wait()
    spot = iota((PG, T), 0)

    def fetch(c, s):
        at = pl.ds(pl.multiple_of(c * 256, 256), 256)
        pltpu.make_async_copy(xr.at[:, at], xcol.at[s], xsem.at[s]).start()
        pltpu.make_async_copy(gr.at[:, at], gcol.at[s], gsem.at[s]).start()

    fetch(0, 0)

    @pl.loop(0, NJ)
    def _(i):
        s = lax.rem(i, 2)

        @pl.when(i + 1 < NJ)
        def _():
            fetch(i + 1, 1 - s)

        landed(xcol.at[s], xsem.at[s])
        landed(gcol.at[s], gsem.at[s])
        at = pl.ds(pl.multiple_of(i * 256, 256), 256)
        xc = xcol[s]
        dg_o[at, :] = dot(xc, gg[...].reshape(ROWS, FF), 0, 0).astype(BF)
        du_o[at, :] = dot(xc, ug[...].reshape(ROWS, FF), 0, 0).astype(BF)
        dd_o[:, at] = dot(hid[...].reshape(ROWS, FF), gcol[s], 0, 0).astype(BF)

        j = lax.rem(own + 4 + i, NJ)
        landed(rrp.at[j], p1r.at[j])
        hots = slots_of(rank_ref, j)
        for c in range(0, DP, 512):
            part[j, :, c : c + 512] = dot(hots, rrp[j, :, c : c + 512], 0, 0).astype(BF)

        @pl.when(i != 4)
        def _():
            send(part.at[j], rrz.at[own], p2s.at[j], p2r.at[own], (grp, j))

        @pl.when(i == 4)
        def _():
            pltpu.make_async_copy(part.at[j], rrz.at[j], p2r.at[j]).start()

        for h in range(2):
            d = 2 * i + h
            a = group_to(grp, d)
            landed(rrq.at[a], t1r.at[a])
            hot = jnp.where(spot == pos_ref[a, 0:1, :], 1.0, 0.0).astype(BF)
            for c in range(0, D - DP, 512):
                s2[a, :, c : c + 512] = dot(hot, rrq[a, :, c : c + 512]).astype(BF)

            if h == 0:
                @pl.when(d > 0)
                def _():
                    send(s2.at[a], rr2.at[grp], t2s.at[a], t2r.at[grp], (a, own))

                @pl.when(d == 0)
                def _():
                    pltpu.make_async_copy(s2.at[a], rr2.at[a], t2r.at[a]).start()
            else:
                send(s2.at[a], rr2.at[grp], t2s.at[a], t2r.at[grp], (a, own))

    for j in range(NJ):
        landed(rrz.at[j], p2r.at[j])
    for c in range(0, DP, 512):
        total = rrz[0, :, c : c + 512].astype(F32)
        for j in range(1, NJ):
            total = total + rrz[j, :, c : c + 512].astype(F32)
        gin_o[:, c : c + 512] = total.astype(BF)
    for a in range(NG):
        landed(rr2.at[a], t2r.at[a])
    for c in range(0, D - DP, 512):
        rows = rr2[:, :, c : c + 512].reshape(NG * PG, 512)
        gin_o[:, DP + c : DP + c + 512] = dot(c_ref[...], rows, 0, 0).astype(BF)

    for a in range(NG):
        landed(dxq.at[a, pl.ds(0, (NJ - 1) * CAP)], t1s.at[a])
    for j in range(NJ):
        landed(dxp.at[j, pl.ds(0, (NG - 1) * CAP)], p1s.at[j])
    for k in range(1, NJ):
        j = lax.rem(own + k, NJ)
        landed(part.at[j], p2s.at[j])
    for d in range(1, NG):
        a = group_to(grp, d)
        landed(s2.at[a], t2s.at[a])


def store_kernel(*refs):
    sems = refs[8]
    copies = []
    for n in range(4):
        size = refs[n].shape[0] // 4
        for q in range(4):
            at = pl.ds(q * size, size)
            copies.append(
                pltpu.make_async_copy(refs[n].at[at], refs[4 + n].at[at], sems.at[n, q])
            )
    for copy in copies:
        copy.start()
    for copy in copies:
        copy.wait()


def body(tokens_in, out_grad, expert_ids, gate_weights, w_gate, w_up, w_down):
    hbm = pl.BlockSpec(memory_space=pl.ANY)
    vm = pl.BlockSpec(memory_space=pltpu.VMEM)
    sem = pltpu.SemaphoreType.DMA
    shape = jax.ShapeDtypeStruct
    wg, wu, wd = w_gate[0], w_up[0], w_down[0]
    xr, gr, hid, gg, ug, hots, pos, rank = pl.pallas_call(
        dispatch_kernel,
        name="dispatch",
        out_shape=(
            shape((NJ, NG, CAP, D), BF), shape((NJ, NG, CAP, D), BF),
            shape((NJ, 2 * T, FF), BF), pltpu.VMEM((NJ, 2 * T, FF), BF),
            pltpu.VMEM((NJ, 2 * T, FF), BF),
            pltpu.VMEM((NG * PG, T), BF), pltpu.VMEM((NG, 8, 128), I32),
            pltpu.VMEM((NJ, NG, T), I32),
        ),
        in_specs=[vm, vm, hbm, vm, hbm, hbm, hbm],
        out_specs=(hbm, hbm, hbm) + (vm,) * 5,
        scratch_shapes=[
            pltpu.VMEM((NJ, T, D), BF),
            pltpu.VMEM((NJ, NG, CAP, D), BF),
            pltpu.VMEM((NG, PG, D), BF),
            pltpu.VMEM((NG, PG, D), BF),
            pltpu.VMEM((NG, NJ * CAP, D), BF),
            pltpu.VMEM((NG, CAP, D), BF),
            pltpu.VMEM((NG, CAP, D), BF),
            pltpu.VMEM((D, FF), BF), pltpu.VMEM((D, FF), BF), pltpu.VMEM((FF, D), BF),
            pltpu.VMEM((2, 2 * T, FF), BF),
            pltpu.VMEM((NJ, NG, T), I32), pltpu.VMEM((NJ, NG, T), I32),
            pltpu.VMEM((NG, 8, 128), I32), pltpu.VMEM((NG, 8, 128), I32),
            pltpu.VMEM((E, T), I32), pltpu.VMEM((E, T), F32),
            sem((7,)), sem((NJ,)), sem((NJ,)), sem((NJ,)),
            sem((NG,)), sem((NG,)), sem((NG,)), sem((NG,)), sem((NG,)), sem((NG,)),
            sem((NG,)), sem((NG,)), sem((3,)), sem((1,)), sem((1,)), sem((2,)),
        ],
        compiler_params=pltpu.CompilerParams(
            collective_id=0, has_side_effects=True, vmem_limit_bytes=48 << 20
        ),
    )(expert_ids.T, gate_weights.T, tokens_in, out_grad, wg, wu, wd)
    grad_in, d_gate, d_up, d_down = pl.pallas_call(
        combine_kernel,
        name="combine",
        out_shape=(
            pltpu.VMEM((T, D), BF), pltpu.VMEM((D, FF), BF),
            pltpu.VMEM((D, FF), BF), pltpu.VMEM((FF, D), BF),
        ),
        in_specs=[vm, vm, vm, hbm, hbm, hbm, vm, vm, hbm, hbm],
        out_specs=(vm, vm, vm, vm),
        scratch_shapes=[
            pltpu.VMEM((NJ, 2 * T, FF), BF),
            pltpu.VMEM((D, FF), BF), pltpu.VMEM((D, FF), BF),
            pltpu.VMEM((NJ, 2 * T, DP), BF),
            pltpu.VMEM((NG, T, D - DP), BF),
            pltpu.VMEM((NJ, 2 * T, DP), BF),
            pltpu.VMEM((NG, T, D - DP), BF),
            pltpu.VMEM((NJ, T, DP), BF),
            pltpu.VMEM((NJ, T, DP), BF),
            pltpu.VMEM((NG, PG, D - DP), BF),
            pltpu.VMEM((NG, PG, D - DP), BF),
            pltpu.VMEM((2, ROWS, 256), BF), pltpu.VMEM((2, ROWS, 256), BF),
            sem((3,)), sem((NJ,)), sem((NJ,)), sem((NJ,)), sem((NJ,)),
            sem((NG,)), sem((NG,)), sem((NG,)), sem((NG,)),
            sem((2,)), sem((2,)),
        ],
        compiler_params=pltpu.CompilerParams(
            collective_id=1, has_side_effects=True, vmem_limit_bytes=42 << 20
        ),
    )(*[pltpu.with_memory_space_constraint(v, pltpu.VMEM) for v in (hots, pos, rank)], xr.reshape(ROWS, D), gr.reshape(ROWS, D), hid,
      *[pltpu.with_memory_space_constraint(v, pltpu.VMEM) for v in (gg, ug)],
      wg, wu)
    outs = [pltpu.with_memory_space_constraint(v, pltpu.VMEM) for v in (grad_in, d_gate, d_up, d_down)]
    grad_in, d_gate, d_up, d_down = pl.pallas_call(
        store_kernel,
        name="store",
        out_shape=tuple(shape(v.shape, BF) for v in outs),
        in_specs=[vm] * 4,
        out_specs=(hbm,) * 4,
        scratch_shapes=[sem((4, 4))],
        compiler_params=pltpu.CompilerParams(vmem_limit_bytes=1 << 20),
    )(*outs)
    return grad_in, d_gate[None], d_up[None], d_down[None]


def solution(mesh):
    both = ("group", "expert")
    return jax.shard_map(
        body,
        mesh=mesh,
        in_specs=(P(both, None),) * 4 + (P(both, None, None),) * 3,
        out_specs=(P(both, None),) + (P(both, None, None),) * 3,
        check_vma=False,
    )
```

```python
import jax
import jax.numpy as jnp
from jax import lax
from jax.experimental import pallas as pl
from jax.experimental.pallas import tpu as pltpu
from jax.sharding import PartitionSpec as P

NG, NJ = 16, 8
T, D, FF = 128, 2048, 768
CAP = 16
PG = 64
E = NG * NJ
DP = 1024
ROWS = NG * NJ * CAP
BF, F32, I32 = jnp.bfloat16, jnp.float32, jnp.int32
MESH = pl.DeviceIdType.MESH
VMEM_LIMIT = 67043328


def dot(a, b, ca=1, cb=0):
    return lax.dot_general(a, b, (((ca,), (cb,)), ((), ())), preferred_element_type=F32)


NEAR = ((0, 1), (1, 0), (0, 3), (3, 0))
DIAG = ((1, 1), (3, 3), (1, 3), (3, 1))
LONG = ((1, 2), (2, 1), (3, 2), (2, 3))
FAR = ((2, 2), (0, 2), (2, 0))
SETS = (NEAR, DIAG, LONG, FAR + ((0, 0),))
OUTWARD = FAR[:1] + LONG + FAR[1:] + DIAG + NEAR


def shift_of(d):
    if isinstance(d, tuple):
        return d
    if isinstance(d, int):
        return d % 4, (d // 4 + d % 4) % 4
    dy = lax.rem(d, 4)
    return dy, lax.rem(lax.div(d, 4) + dy, 4)


def group_to(grp, d):
    dy, dx = shift_of(d)
    return lax.rem(lax.div(grp, 4) + dy, 4) * 4 + lax.rem(lax.rem(grp, 4) + dx, 4)


def group_from(grp, d):
    dy, dx = shift_of(d)
    return lax.rem(lax.div(grp, 4) - dy + 4, 4) * 4 + lax.rem(lax.rem(grp, 4) - dx + 4, 4)


def enter(grp, own):
    barrier = pltpu.get_barrier_semaphore()
    for d in range(1, NG):
        pl.semaphore_signal(barrier, inc=1, device_id=(group_to(grp, d), own), device_id_type=MESH)
    for k in range(1, NJ):
        pl.semaphore_signal(
            barrier, inc=1, device_id=(grp, lax.rem(own + k, NJ)), device_id_type=MESH
        )
    return barrier


def send(src, dst, ssem, rsem, device):
    pltpu.make_async_remote_copy(
        src_ref=src, dst_ref=dst, send_sem=ssem, recv_sem=rsem,
        device_id=device, device_id_type=MESH,
    ).start()


def landed(ref, sem):
    pltpu.make_async_copy(ref, ref, sem).wait()


def iota(shape, dim):
    return lax.broadcasted_iota(I32, shape, dim)


def slots_of(rank_ref, j):
    spot = iota((CAP, T), 0)
    return jnp.concatenate(
        [jnp.where(spot == rank_ref[j, a : a + 1, :], 1.0, 0.0).astype(BF) for a in range(NG)],
        axis=0,
    )


def dispatch_kernel(
    ids_ref, gw_ref, x_hbm, g_ref, wg_hbm, wu_hbm, wd_hbm,
    xr, gr, hid_o, gg_o, ug_o, c_o, pos_o, rank_o,
    ax, pbuf, s1, r1, s2, stx, stg, wg, wu, wd, ost,
    rank_s, rank_r, pos_s, pos_r, post, wt,
    axs, axr, ms, mr, ps, pr, q1s, q1r, q2s, q2r, p2s, p2r, wsem, xsem, gsem, osem,
):
    grp, own = lax.axis_index("group"), lax.axis_index("expert")
    partner = own + 1 - 2 * lax.rem(own, 2)
    barrier = enter(grp, own)
    loads = [
        pltpu.make_async_copy(wg_hbm, wg, wsem.at[0]),
        pltpu.make_async_copy(wu_hbm, wu, wsem.at[1]),
        pltpu.make_async_copy(wd_hbm, wd, wsem.at[2]),
    ]
    pltpu.make_async_copy(x_hbm, ax.at[own], axr.at[own]).start()

    row, lane = iota((E, T), 0), iota((E, T), 1)
    before = jnp.where(row < lane, 1.0, 0.0).astype(BF)
    named = jnp.zeros((E, T), F32)
    weight = jnp.zeros((E, T), F32)
    named_p = jnp.zeros((E, T), F32)
    row_p = lax.rem(row, NG) * NJ + lax.div(row, NG)
    for k in range(8):
        idk = ids_ref[k : k + 1, :]
        gwk = gw_ref[k : k + 1, :]
        named = jnp.where(row == idk, 1.0, named)
        weight = jnp.where(row == idk, gwk, weight)
        named_p = jnp.where(row_p == idk, 1.0, named_p)
    rank = dot(named.astype(BF), before)
    rank_p = dot(named_p.astype(BF), before)
    counts = dot(named.astype(BF), jnp.ones((T, T), BF))
    ahead = jnp.where(
        (lax.div(row, NJ) == lax.div(lane, NJ)) & (lane < row), 1.0, 0.0
    ).astype(BF)
    starts = dot(ahead, counts.astype(BF))
    post[...] = jnp.where(named > 0.5, starts + rank, -1.0).astype(I32)
    wt[...] = weight
    rank_s[...] = jnp.where(named_p > 0.5, rank_p, -1.0).astype(I32).reshape(NJ, NG, T)
    mine = lax.rem(row, NJ) == lax.div(lane, CAP)
    pick = jnp.where(lax.div(iota((NG, E), 1), NJ) == iota((NG, E), 0), 1.0, 0.0).astype(BF)
    start_row = dot(pick, jnp.where(mine, starts, 0.0).astype(BF))
    count_row = dot(pick, jnp.where(mine, counts, 0.0).astype(BF))
    slot = lax.rem(iota((NG, E), 1), CAP).astype(F32)
    pos = jnp.where(slot < count_row, start_row + slot, -1.0).astype(I32)
    for a in range(NG):
        pos_s[a] = jnp.broadcast_to(pos[a : a + 1, :], (8, 128))
    rank_r[own] = rank_s[own]
    pos_r[grp] = pos_s[grp]

    pl.semaphore_wait(barrier, NG + NJ - 2)

    for k in range(1, NJ):
        to = lax.rem(own + k, NJ)
        send(rank_s.at[to], rank_r.at[own], ms.at[k], mr.at[own], (grp, to))
    for i in range(1, 4):
        to = lax.rem(own + 2 * i, NJ)
        send(x_hbm, ax.at[own], axs.at[i], axr.at[own], (grp, to))
    send(x_hbm, ax.at[own], axs.at[0], axr.at[own], (grp, partner))

    spot = iota((PG, T), 0)
    for steps in SETS:
        picks, scales = [], []
        for d in steps:
            a = group_to(grp, d)
            at = pl.ds(pl.multiple_of(a * NJ, NJ), NJ)
            prow, wrow = post[at, :], wt[at, :]
            hot = jnp.zeros((PG, T), F32)
            wsel = jnp.zeros((PG, T), F32)
            for e in range(NJ):
                hit = spot == prow[e : e + 1, :]
                hot = jnp.where(hit, 1.0, hot)
                wsel = jnp.where(hit, wrow[e : e + 1, :], wsel)
            c_o[pl.ds(pl.multiple_of(a * PG, PG), PG), :] = hot.astype(BF)
            picks.append(hot.astype(BF))
            scales.append(jnp.sum(wsel, axis=1, keepdims=True))
        hots = jnp.concatenate(picks, axis=0)
        scale = jnp.concatenate(scales, axis=0)
        for c in range(0, D, 512):
            part = (scale * dot(hots, g_ref[:, c : c + 512])).astype(BF)
            for q, d in enumerate(steps):
                s1[group_to(grp, d), :, c : c + 512] = part[q * PG : (q + 1) * PG, :]
        ends = [d for d in steps if d != (0, 0)]
        for d in ends:
            a = group_to(grp, d)
            send(pos_s.at[a], pos_r.at[grp], ps.at[a], pr.at[grp], (a, own))
        for r in range(0, PG, 16):
            for d in ends:
                a = group_to(grp, d)
                send(s1.at[a, pl.ds(r, 16)], r1.at[grp, pl.ds(r, 16)],
                     q1s.at[a], q1r.at[grp], (a, own))
    for w in loads:
        w.start()

    def spread(a, rows_ref):
        hot = jnp.where(spot == pos_r[a, 0:1, :], 1.0, 0.0).astype(BF)
        for c in range(0, D, 512):
            s2[a, :, c : c + 512] = dot(hot, rows_ref[a, :, c : c + 512], 0, 0).astype(BF)
        for k in range(1, NJ):
            to = lax.rem(own + k, NJ)
            at = pl.ds(pl.multiple_of(to * CAP, CAP), CAP)
            send(s2.at[a, at], gr.at[own, a], q2s.at[a], q2r.at[own], (grp, to))
        at = pl.ds(pl.multiple_of(own * CAP, CAP), CAP)
        pltpu.make_async_copy(s2.at[a, at], gr.at[own, a], q2r.at[own]).start()

    spread(grp, s1)

    for k in range(1, NJ):
        frm = lax.rem(own + k, NJ)
        landed(rank_r.at[frm], mr.at[frm])

    def source(n):
        side = lax.rem(n, 2)
        return lax.rem(own + (partner - own) * side - (n - side) + NJ, NJ)

    @pl.loop(0, NJ)
    def _(n):
        j = source(n)
        landed(ax.at[j], axr.at[j])

        @pl.when((n >= 2) & (lax.rem(n, 2) == 0))
        def _():
            send(ax.at[j], ax.at[j], axs.at[3 + lax.div(n, 2)], axr.at[j], (grp, partner))

        hots = slots_of(rank_r, j)
        for c in range(0, D, 512):
            part = dot(hots, ax[j, :, c : c + 512]).astype(BF)
            pbuf[j, :, :, c : c + 512] = part.reshape(NG, CAP, 512)
        for d in OUTWARD:
            a = group_to(grp, d)
            send(pbuf.at[j, a], xr.at[j, grp], p2s.at[j], p2r.at[j], (a, own))
        pltpu.make_async_copy(pbuf.at[j, grp], xr.at[j, grp], p2r.at[j]).start()

    for steps in SETS:
        for d in steps:
            if d != (0, 0):
                a = group_from(grp, d)
                landed(pos_r.at[a], pr.at[a])
                landed(r1.at[a], q1r.at[a])
                spread(a, r1)

    for w in loads:
        w.wait()

    @pl.loop(0, NJ)
    def _(n):
        j = source(n)
        landed(xr.at[j], p2r.at[j])
        landed(gr.at[j], q2r.at[j])
        x_in = pltpu.make_async_copy(xr.at[j], stx, xsem.at[0])
        g_in = pltpu.make_async_copy(gr.at[j], stg, gsem.at[0])
        x_in.start()
        g_in.start()
        x_in.wait()
        g_in.wait()
        xb = stx[...].reshape(2 * T, D)
        gate_pre = dot(xb, wg[...])
        up_pre = dot(xb, wu[...])
        hgrad = dot(stg[...].reshape(2 * T, D), wd[...], 1, 1)
        sigma = jax.nn.sigmoid(gate_pre)
        act = gate_pre * sigma
        slot_n = lax.rem(n, 2)

        @pl.when(n >= 2)
        def _():
            landed(ost.at[slot_n], osem.at[slot_n])

        ost[slot_n] = (act * up_pre).astype(BF)
        pltpu.make_async_copy(ost.at[slot_n], hid_o.at[j], osem.at[slot_n]).start()
        gg_o[j] = (hgrad * up_pre * sigma * (1.0 + gate_pre * (1.0 - sigma))).astype(BF)
        ug_o[j] = (hgrad * act).astype(BF)

    for n in range(2):
        landed(ost.at[n], osem.at[n])
    pos_o[...] = pos_r[...]
    rank_o[...] = rank_r[...]
    for k in range(1, NJ):
        to = lax.rem(own + k, NJ)
        landed(rank_s.at[to], ms.at[k])
    for i in range(7):
        landed(x_hbm, axs.at[i])
    for d in range(1, NG):
        a = group_to(grp, d)
        landed(pos_s.at[a], ps.at[a])
        landed(s1.at[a], q1s.at[a])
    for j in range(NJ):
        landed(pbuf.at[j, pl.ds(0, NG - 1)], p2s.at[j])
    for a in range(NG):
        landed(s2.at[a, pl.ds(0, (NJ - 1) * CAP)], q2s.at[a])


def combine_kernel(
    pos_ref, rank_ref, xr, gr, hid_hbm, gg, ug, wg_hbm, wu_hbm,
    dg_o, du_o, dd_o, rrz, rr2,
    hid, wg, wu, dxp, dxq, rrp, rrq, part, s2, xcol, gcol,
    wsem, p1s, p1r, p2s, p2r, t1s, t1r, t2s, t2r, xsem, gsem,
):
    grp, own = lax.axis_index("group"), lax.axis_index("expert")
    barrier = enter(grp, own)
    loads = [
        pltpu.make_async_copy(wg_hbm, wg, wsem.at[0]),
        pltpu.make_async_copy(wu_hbm, wu, wsem.at[1]),
        pltpu.make_async_copy(hid_hbm, hid, wsem.at[2]),
    ]
    for w in loads:
        w.start()
    for w in loads[:2]:
        w.wait()

    def slot_rows(a):
        return pl.ds(pl.multiple_of(a * CAP, CAP), CAP)

    def input_rows(ggb, ugb, c):
        return (
            dot(ggb, wg[c : c + 512, :], 1, 1) + dot(ugb, wu[c : c + 512, :], 1, 1)
        ).astype(BF)

    def make_rows(n):
        j = lax.rem(own + 4 + n, NJ)
        for c in range(0, DP, 512):
            dxp[j, :, c : c + 512] = input_rows(gg[j], ug[j], c)
        tops = [group_to(grp, 2 * n + h) for h in range(2)]
        ats = [slot_rows(a) for a in tops]
        ggb = jnp.concatenate([gg[q, at, :] for at in ats for q in range(NJ)], axis=0)
        ugb = jnp.concatenate([ug[q, at, :] for at in ats for q in range(NJ)], axis=0)
        for c in range(DP, D, 512):
            rows = input_rows(ggb, ugb, c)
            for h in range(2):
                dxq[tops[h], :, c - DP : c - DP + 512] = rows[h * T : (h + 1) * T, :]

    def send_rows(n):
        j = lax.rem(own + 4 + n, NJ)
        for d in OUTWARD:
            a = group_to(grp, d)
            send(dxp.at[j, slot_rows(a)], rrp.at[j, slot_rows(grp)],
                 p1s.at[j], p1r.at[j], (a, own))
        pltpu.make_async_copy(
            dxp.at[j, slot_rows(grp)], rrp.at[j, slot_rows(grp)], p1r.at[j]
        ).start()
        for h in range(2):
            a = group_to(grp, 2 * n + h)
            for k in range(1, NJ):
                to = lax.rem(own + k, NJ)
                send(dxq.at[a, slot_rows(to)], rrq.at[a, slot_rows(own)],
                     t1s.at[a], t1r.at[a], (grp, to))
            pltpu.make_async_copy(
                dxq.at[a, slot_rows(own)], rrq.at[a, slot_rows(own)], t1r.at[a]
            ).start()

    make_rows(0)
    pl.semaphore_wait(barrier, NG + NJ - 2)
    send_rows(0)

    @pl.loop(1, NJ)
    def _(n):
        make_rows(n)
        send_rows(n)

    loads[2].wait()
    spot = iota((PG, T), 0)

    def fetch(c, s):
        at = pl.ds(pl.multiple_of(c * 256, 256), 256)
        pltpu.make_async_copy(xr.at[:, at], xcol.at[s], xsem.at[s]).start()
        pltpu.make_async_copy(gr.at[:, at], gcol.at[s], gsem.at[s]).start()

    fetch(0, 0)

    @pl.loop(0, NJ)
    def _(i):
        s = lax.rem(i, 2)

        @pl.when(i + 1 < NJ)
        def _():
            fetch(i + 1, 1 - s)

        landed(xcol.at[s], xsem.at[s])
        landed(gcol.at[s], gsem.at[s])
        at = pl.ds(pl.multiple_of(i * 256, 256), 256)
        xc = xcol[s]
        dg_o[at, :] = dot(xc, gg[...].reshape(ROWS, FF), 0, 0).astype(BF)
        du_o[at, :] = dot(xc, ug[...].reshape(ROWS, FF), 0, 0).astype(BF)
        dd_o[:, at] = dot(hid[...].reshape(ROWS, FF), gcol[s], 0, 0).astype(BF)

        j = lax.rem(own + 4 + i, NJ)
        landed(rrp.at[j], p1r.at[j])
        hots = slots_of(rank_ref, j)
        for c in range(0, DP, 512):
            part[j, :, c : c + 512] = dot(hots, rrp[j, :, c : c + 512], 0, 0).astype(BF)

        @pl.when(i != 4)
        def _():
            send(part.at[j], rrz.at[own], p2s.at[j], p2r.at[own], (grp, j))

        @pl.when(i == 4)
        def _():
            pltpu.make_async_copy(part.at[j], rrz.at[j], p2r.at[j]).start()

        for h in range(2):
            d = 2 * i + h
            a = group_to(grp, d)
            landed(rrq.at[a], t1r.at[a])
            hot = jnp.where(spot == pos_ref[a, 0:1, :], 1.0, 0.0).astype(BF)
            for c in range(0, D - DP, 512):
                s2[a, :, c : c + 512] = dot(hot, rrq[a, :, c : c + 512]).astype(BF)

            if h == 0:
                @pl.when(d > 0)
                def _():
                    send(s2.at[a], rr2.at[grp], t2s.at[a], t2r.at[grp], (a, own))

                @pl.when(d == 0)
                def _():
                    pltpu.make_async_copy(s2.at[a], rr2.at[a], t2r.at[a]).start()
            else:
                send(s2.at[a], rr2.at[grp], t2s.at[a], t2r.at[grp], (a, own))

    for j in range(NJ):
        landed(rrz.at[j], p2r.at[j])
    for a in range(NG):
        landed(rr2.at[a], t2r.at[a])
    for a in range(NG):
        landed(dxq.at[a, pl.ds(0, (NJ - 1) * CAP)], t1s.at[a])
    for j in range(NJ):
        landed(dxp.at[j, pl.ds(0, (NG - 1) * CAP)], p1s.at[j])
    for k in range(1, NJ):
        j = lax.rem(own + k, NJ)
        landed(part.at[j], p2s.at[j])
    for d in range(1, NG):
        a = group_to(grp, d)
        landed(s2.at[a], t2s.at[a])


def store_kernel(c_ref, rrz, rr2, dg, du, dd, gin_o, dg_o, du_o, dd_o, gin, sems, gsem):
    copies = []
    for n, (src, dst) in enumerate(((dg, dg_o), (du, du_o), (dd, dd_o))):
        size = src.shape[0] // 4
        for q in range(4):
            at = pl.ds(q * size, size)
            copies.append(pltpu.make_async_copy(src.at[at], dst.at[at], sems.at[n, q]))
    for copy in copies:
        copy.start()
    for c in range(0, DP, 512):
        total = rrz[0, :, c : c + 512].astype(F32)
        for j in range(1, NJ):
            total = total + rrz[j, :, c : c + 512].astype(F32)
        gin[:, c : c + 512] = total.astype(BF)
    for c in range(0, D - DP, 512):
        rows = rr2[:, :, c : c + 512].reshape(NG * PG, 512)
        gin[:, DP + c : DP + c + 512] = dot(c_ref[...], rows, 0, 0).astype(BF)
    last = pltpu.make_async_copy(gin, gin_o, gsem.at[0])
    last.start()
    for copy in copies:
        copy.wait()
    last.wait()


def body(tokens_in, out_grad, expert_ids, gate_weights, w_gate, w_up, w_down):
    hbm = pl.BlockSpec(memory_space=pl.ANY)
    vm = pl.BlockSpec(memory_space=pltpu.VMEM)
    sem = pltpu.SemaphoreType.DMA
    shape = jax.ShapeDtypeStruct
    wg, wu, wd = w_gate[0], w_up[0], w_down[0]
    xr, gr, hid, gg, ug, hots, pos, rank = pl.pallas_call(
        dispatch_kernel,
        name="dispatch",
        out_shape=(
            shape((NJ, NG, CAP, D), BF), shape((NJ, NG, CAP, D), BF),
            shape((NJ, 2 * T, FF), BF), pltpu.VMEM((NJ, 2 * T, FF), BF),
            pltpu.VMEM((NJ, 2 * T, FF), BF),
            pltpu.VMEM((NG * PG, T), BF), pltpu.VMEM((NG, 8, 128), I32),
            pltpu.VMEM((NJ, NG, T), I32),
        ),
        in_specs=[vm, vm, hbm, vm, hbm, hbm, hbm],
        out_specs=(hbm, hbm, hbm) + (vm,) * 5,
        scratch_shapes=[
            pltpu.VMEM((NJ, T, D), BF),
            pltpu.VMEM((NJ, NG, CAP, D), BF),
            pltpu.VMEM((NG, PG, D), BF),
            pltpu.VMEM((NG, PG, D), BF),
            pltpu.VMEM((NG, NJ * CAP, D), BF),
            pltpu.VMEM((NG, CAP, D), BF),
            pltpu.VMEM((NG, CAP, D), BF),
            pltpu.VMEM((D, FF), BF), pltpu.VMEM((D, FF), BF), pltpu.VMEM((FF, D), BF),
            pltpu.VMEM((2, 2 * T, FF), BF),
            pltpu.VMEM((NJ, NG, T), I32), pltpu.VMEM((NJ, NG, T), I32),
            pltpu.VMEM((NG, 8, 128), I32), pltpu.VMEM((NG, 8, 128), I32),
            pltpu.VMEM((E, T), I32), pltpu.VMEM((E, T), F32),
            sem((7,)), sem((NJ,)), sem((NJ,)), sem((NJ,)),
            sem((NG,)), sem((NG,)), sem((NG,)), sem((NG,)), sem((NG,)), sem((NG,)),
            sem((NG,)), sem((NG,)), sem((3,)), sem((1,)), sem((1,)), sem((2,)),
        ],
        compiler_params=pltpu.CompilerParams(
            collective_id=0, has_side_effects=True, vmem_limit_bytes=48 << 20
        ),
    )(expert_ids.T, gate_weights.T, tokens_in, out_grad, wg, wu, wd)
    d_gate, d_up, d_down, sums, rows = pl.pallas_call(
        combine_kernel,
        name="combine",
        out_shape=(
            pltpu.VMEM((D, FF), BF), pltpu.VMEM((D, FF), BF), pltpu.VMEM((FF, D), BF),
            pltpu.VMEM((NJ, T, DP), BF), pltpu.VMEM((NG, PG, D - DP), BF),
        ),
        in_specs=[vm, vm, hbm, hbm, hbm, vm, vm, hbm, hbm],
        out_specs=(vm,) * 5,
        scratch_shapes=[
            pltpu.VMEM((NJ, 2 * T, FF), BF),
            pltpu.VMEM((D, FF), BF), pltpu.VMEM((D, FF), BF),
            pltpu.VMEM((NJ, 2 * T, DP), BF),
            pltpu.VMEM((NG, T, D - DP), BF),
            pltpu.VMEM((NJ, 2 * T, DP), BF),
            pltpu.VMEM((NG, T, D - DP), BF),
            pltpu.VMEM((NJ, T, DP), BF),
            pltpu.VMEM((NG, PG, D - DP), BF),
            pltpu.VMEM((2, ROWS, 256), BF), pltpu.VMEM((2, ROWS, 256), BF),
            sem((3,)), sem((NJ,)), sem((NJ,)), sem((NJ,)), sem((NJ,)),
            sem((NG,)), sem((NG,)), sem((NG,)), sem((NG,)),
            sem((2,)), sem((2,)),
        ],
        compiler_params=pltpu.CompilerParams(
            collective_id=1, has_side_effects=True, vmem_limit_bytes=38 << 20
        ),
    )(*[pltpu.with_memory_space_constraint(v, pltpu.VMEM) for v in (pos, rank)], xr.reshape(ROWS, D), gr.reshape(ROWS, D), hid,
      *[pltpu.with_memory_space_constraint(v, pltpu.VMEM) for v in (gg, ug)],
      wg, wu)
    grad_in, d_gate, d_up, d_down = pl.pallas_call(
        store_kernel,
        name="store",
        out_shape=(
            shape((T, D), BF), shape((D, FF), BF), shape((D, FF), BF), shape((FF, D), BF),
        ),
        in_specs=[vm] * 6,
        out_specs=(hbm,) * 4,
        scratch_shapes=[pltpu.VMEM((T, D), BF), sem((3, 4)), sem((1,))],
        compiler_params=pltpu.CompilerParams(vmem_limit_bytes=4 << 20),
    )(*[
        pltpu.with_memory_space_constraint(v, pltpu.VMEM)
        for v in (hots, sums, rows, d_gate, d_up, d_down)
    ])
    return grad_in, d_gate[None], d_up[None], d_down[None]


def solution(mesh):
    both = ("group", "expert")
    return jax.shard_map(
        body,
        mesh=mesh,
        in_specs=(P(both, None),) * 4 + (P(both, None, None),) * 3,
        out_specs=(P(both, None),) + (P(both, None, None),) * 3,
        check_vma=False,
    )
```
